128 devices in a mesh: outer: 16 (over x, z), inner: 8 (over y, core).
Axes of the slice: x: 4, y: 4, z: 4, core: 2. Of those that a mesh axis runs over, the one named last changes fastest.
Arguments:
- queries: bfloat16 [16384, 4096], P(('outer', 'inner')), may hold values from -170 to 170
- keys: bfloat16 [16384, 4096], P(('outer', 'inner')), may hold values from -170 to 170
- values: bfloat16 [16384, 4096], P(('outer', 'inner')), may hold values from -5 to 5
- teacher: bfloat16 [16384, 4096], P(('outer', 'inner')), may hold values from -12 to 12
- query_map: bfloat16 [32, 64, 128], replicated, may hold values from -0.5 to 0.5
- key_map: bfloat16 [32, 64, 128], replicated, may hold values from -0.5 to 0.5
Outputs:
- attn_out: bfloat16 [16384, 4096], P(('outer', 'inner'))
- loss: float32 [], replicated
- grad_query_map: float32 [32, 64, 128], replicated
- grad_key_map: float32 [32, 64, 128], replicated
The draws below stay inside these ranges and needn't reach their ends.
All inputs are finite; a program needn't handle non-finite values.
Results may differ from the reference program's by a relative error of at most 0.011.
Values sent between devices are 32-bit elements; how exact they have to be, the bound alone decides.
No kernel may reach another device: no remote copies, remote signals or barrier semaphores. Data moves between devices by JAX's collectives and lax.ppermute only.
A program may use at most 512 MiB of HBM per device.

```python
import jax
import jax.numpy as jnp
from jax import lax

DH = 128
H = 32
FD = 64
TOK_DEV = 128
TOKENS = 16384


def draw_queries(key, part):
    key = jax.random.fold_in(key, 11)
    first = jax.random.fold_in(key, 0)
    shape = (TOKENS, H * DH)
    base = 2.0 * jnp.clip(jax.random.normal(first, shape, jnp.float32), -4.0, 4.0)
    return base.astype(jnp.bfloat16)


def draw_keys(key, part):
    key = jax.random.fold_in(key, 12)
    first = jax.random.fold_in(key, 0)
    shape = (TOKENS, H * DH)
    base = 2.0 * jnp.clip(jax.random.normal(first, shape, jnp.float32), -4.0, 4.0)
    return base.astype(jnp.bfloat16)


def draw_values(key, part):
    key = jax.random.fold_in(key, 13)
    first, second = jax.random.split(key)
    blocks = TOKENS // TOK_DEV
    offsets = jax.random.uniform(second, (blocks, 1, H * DH), jnp.float32, -1.0, 1.0)
    noise = jnp.clip(jax.random.normal(first, (blocks, TOK_DEV, H * DH), jnp.float32), -4.0, 4.0)
    return (noise + offsets).reshape(TOKENS, H * DH).astype(jnp.bfloat16)


def draw_teacher(key, part):
    key = jax.random.fold_in(key, 14)
    rows = jnp.arange(TOKENS, dtype=jnp.float32)[:, None]
    scale = 1.0 + 2.0 * rows / TOKENS
    shape = (TOKENS, H * DH)
    base = jnp.clip(jax.random.normal(key, shape, jnp.float32), -4.0, 4.0)
    return (base * scale).astype(jnp.bfloat16)


def scatter_about(rng, shape, spread, limit, kind=jnp.bfloat16):
    drawn = jax.random.normal(rng, shape, jnp.float32) * spread
    return jnp.minimum(jnp.maximum(drawn, -limit), limit).astype(kind)


def setup_inputs(seed: int = 0) -> dict:
    arg_keys = jax.random.split(jax.random.key(seed), 7)
    return {
        "queries": draw_queries(jax.random.fold_in(arg_keys[6], 71), 0),
        "keys": draw_keys(jax.random.fold_in(arg_keys[6], 71), 0),
        "values": draw_values(jax.random.fold_in(arg_keys[6], 71), 0),
        "teacher": draw_teacher(jax.random.fold_in(arg_keys[6], 71), 0),
        "query_map": scatter_about(arg_keys[4], (H, FD, DH), DH ** -0.5, 0.5),
        "key_map": scatter_about(arg_keys[5], (H, FD, DH), DH ** -0.5, 0.5),
    }


hp = lax.Precision.HIGHEST


def feature_map(x, w):
    logits = jnp.einsum('thd,hfd->thf', x.astype(jnp.float32), w.astype(jnp.float32), precision=hp)
    first = jax.nn.softmax(logits, axis=-1)
    second = jax.nn.softmax(-logits, axis=-1)
    return jnp.concatenate([first, second], axis=-1), first, second


def soft_back(dphi, first, second, x):
    half = first.shape[-1]
    part_one = dphi[..., :half]
    part_two = dphi[..., half:]
    grad_logit = first * (part_one - jnp.sum(first * part_one, -1, keepdims=True))
    grad_logit = grad_logit - second * (part_two - jnp.sum(second * part_two, -1, keepdims=True))
    grad_b = grad_logit.astype(jnp.bfloat16).astype(jnp.float32)
    return jnp.einsum('thf,thd->hfd', grad_b, x.astype(jnp.float32), precision=hp)


def local_states(key_blk, val_blk, key_map):
    phik, first, second = feature_map(key_blk, key_map)
    phikb = phik.astype(jnp.bfloat16).astype(jnp.float32)
    state = jnp.einsum('thf,thd->hfd', phikb, val_blk.astype(jnp.float32), precision=hp)
    return state, jnp.sum(phik, axis=0)


def reference(queries, keys, values, teacher, query_map, key_map):
    blocks = TOKENS // TOK_DEV
    shape = (blocks, TOK_DEV, H, DH)
    q_all = queries.reshape(shape)
    k_all = keys.reshape(shape)
    v_all = values.reshape(shape)
    t_all = teacher.reshape(shape)
    zero_state = jnp.zeros((H, 2 * FD, DH), jnp.float32)
    zero_norm = jnp.zeros((H, 2 * FD), jnp.float32)

    def forward_step(carry, item):
        key_blk, val_blk = item
        state, norm = local_states(key_blk, val_blk, key_map)
        return (carry[0] + state, carry[1] + norm), carry

    _, prefixes = lax.scan(forward_step, (zero_state, zero_norm), (k_all, v_all))
    mask = jnp.tril(jnp.ones((TOK_DEV, TOK_DEV), jnp.float32))

    def backward_step(carry, item):
        rev_suf, rnorm_suf, grad_q, grad_k, total = carry
        q_blk, k_blk, v_blk, t_blk, state_pre, norm_pre = item
        phiq, aq, bq = feature_map(q_blk, query_map)
        phik, ak, bk = feature_map(k_blk, key_map)
        phiqb = phiq.astype(jnp.bfloat16).astype(jnp.float32)
        phikb = phik.astype(jnp.bfloat16).astype(jnp.float32)
        vf = v_blk.astype(jnp.float32)
        scores = jnp.einsum('thf,shf->hts', phiqb, phikb, precision=hp) * mask[None]
        scoresb = scores.astype(jnp.bfloat16).astype(jnp.float32)
        preb = state_pre.astype(jnp.bfloat16).astype(jnp.float32)
        num = jnp.einsum('hts,shd->thd', scoresb, vf, precision=hp) + jnp.einsum('thf,hfd->thd', phiqb, preb, precision=hp)
        den = jnp.sum(scores, axis=2).T + jnp.einsum('thf,hf->th', phiq, norm_pre, precision=hp)
        y = num / den[..., None]
        err = y - t_blk.astype(jnp.float32)
        total = total + jnp.sum(err * err) / (H * DH)
        grad_out = (2.0 / (H * DH)) * err
        dnum = grad_out / den[..., None]
        dnumb = dnum.astype(jnp.bfloat16).astype(jnp.float32)
        dden = -jnp.sum(grad_out * y, axis=-1) / den
        rev_loc = jnp.einsum('thf,thd->hfd', phiqb, dnumb, precision=hp)
        rnorm_loc = jnp.einsum('thf,th->hf', phiq, dden, precision=hp)
        grid = (jnp.einsum('thd,shd->hts', dnumb, vf, precision=hp) + dden.T[:, :, None]) * mask[None]
        gridb = grid.astype(jnp.bfloat16).astype(jnp.float32)
        revb = rev_suf.astype(jnp.bfloat16).astype(jnp.float32)
        dphiq = jnp.einsum('hts,shf->thf', gridb, phikb, precision=hp) + jnp.einsum('thd,hfd->thf', dnumb, preb, precision=hp) + dden[..., None] * norm_pre[None]
        dphik = jnp.einsum('hts,thf->shf', gridb, phiqb, precision=hp) + jnp.einsum('shd,hfd->shf', vf, revb, precision=hp) + rnorm_suf[None]
        grad_q = grad_q + soft_back(dphiq, aq, bq, q_blk)
        grad_k = grad_k + soft_back(dphik, ak, bk, k_blk)
        new_carry = (rev_suf + rev_loc, rnorm_suf + rnorm_loc, grad_q, grad_k, total)
        return new_carry, y.astype(jnp.bfloat16)

    zero_grad = jnp.zeros((H, FD, DH), jnp.float32)
    init = (zero_state, zero_norm, zero_grad, zero_grad, jnp.zeros((), jnp.float32))
    final, outs = lax.scan(backward_step, init, (q_all, k_all, v_all, t_all, prefixes[0], prefixes[1]), reverse=True)
    attn_out = outs.reshape(TOKENS, H * DH)
    loss = final[4] / TOKENS
    return attn_out, loss, final[2], final[3]
```

```python
import functools

import jax
import jax.numpy as jnp
from jax import lax
from jax.experimental import pallas as pl
from jax.experimental.pallas import tpu as pltpu
from jax.sharding import Mesh
from jax.sharding import PartitionSpec as P

F32 = jnp.float32
BF16 = jnp.bfloat16
CHIPS = ("x", "z", "y")
NCHIP = 64
HEADS = 32
HALF = 16
ROWS = 128
TOK = 256
GRP = 4
STEPS = HALF // GRP
PIECE = 33
GROWS = GRP * 4 * PIECE
ALL_ROWS = HALF * 4 * PIECE
WIDTH = 128


def dot(a, b, dims):
    return lax.dot_general(a, b, (dims, ((), ())), preferred_element_type=F32)


def low_lanes(shape):
    return lax.broadcasted_iota(jnp.int32, shape, 1) < 64


def halves_sum(x, low):
    first = jnp.sum(jnp.where(low, x, 0.0), axis=1, keepdims=True)
    second = jnp.sum(jnp.where(low, 0.0, x), axis=1, keepdims=True)
    return first, second


def feature_map(x, w):
    signed = jnp.concatenate([w, -w], axis=0)
    logits = dot(x, signed, ((1,), (1,)))
    low = low_lanes(logits.shape)
    big = jnp.float32(-3e38)
    top_one = jnp.max(jnp.where(low, logits, big), axis=1, keepdims=True)
    top_two = jnp.max(jnp.where(low, big, logits), axis=1, keepdims=True)
    e = jnp.exp(logits - jnp.where(low, top_one, top_two))
    sum_one, sum_two = halves_sum(e, low)
    return e * jnp.where(low, 1.0 / sum_one, 1.0 / sum_two)


def soft_back(phi, dphi, x):
    low = low_lanes(phi.shape)
    sum_one, sum_two = halves_sum(phi * dphi, low)
    d = phi * (dphi - jnp.where(low, sum_one, sum_two))
    dlogit = (d - pltpu.roll(d, 64, 1)).astype(BF16)
    return dot(dlogit, x, ((0,), (0,)))[:64]


def both_cores(core, own, other, buf):
    buf[pl.ds(pl.multiple_of(core * ROWS, ROWS), ROWS), :] = own
    buf[pl.ds(pl.multiple_of((1 - core) * ROWS, ROWS), ROWS), :] = other.astype(BF16)
    return buf[...]


def put_state(ref, i, state, row):
    for q in range(4):
        at = (4 * i + q) * PIECE
        ref[at : at + 32, :] = state[32 * q : 32 * q + 32]
        ref[at + 32 : at + 33, :] = row


def get_state(ref, i):
    parts = [ref[(4 * i + q) * PIECE : (4 * i + q) * PIECE + 32, :] for q in range(4)]
    at = 4 * i * PIECE + 32
    return jnp.concatenate(parts, axis=0), ref[at : at + 1, :]


def key_kernel(core_ref, k_own, k_other, v_own, v_other, w_ref, kf, vf, phik_ref, send, kbuf, vbuf):
    core = core_ref[0]
    for i in range(GRP):
        cols = slice(WIDTH * i, WIDTH * (i + 1))
        k = both_cores(core, k_own[:, cols], k_other[:, cols], kbuf.at[i])
        v = both_cores(core, v_own[:, cols], v_other[:, cols], vbuf.at[i])
        kf[:, cols] = k
        vf[:, cols] = v
        phik = feature_map(k, w_ref[i])
        phik_ref[:, cols] = phik
        state = dot(phik.astype(BF16), v, ((0,), (0,)))
        put_state(send, i, state, jnp.sum(phik, axis=0, keepdims=True))


def query_kernel(
    core_ref, q_own, q_other, t_own, t_other, w_ref, phik_ref, vf, pre,
    y_own, y_send, send, dphik_ref, grad_ref, loss_ref, qbuf, tbuf, ybuf,
):
    core = core_ref[0]

    @pl.when(pl.program_id(0) == 0)
    def _():
        loss_ref[...] = jnp.zeros_like(loss_ref)

    mask = lax.broadcasted_iota(jnp.int32, (TOK, TOK), 0) >= lax.broadcasted_iota(
        jnp.int32, (TOK, TOK), 1
    )
    mine = pl.ds(pl.multiple_of(core * ROWS, ROWS), ROWS)
    theirs = pl.ds(pl.multiple_of((1 - core) * ROWS, ROWS), ROWS)
    scale = 2.0 / (HEADS * WIDTH)
    for i in range(GRP):
        cols = slice(WIDTH * i, WIDTH * (i + 1))
        q = both_cores(core, q_own[:, cols], q_other[:, cols], qbuf.at[i])
        t = both_cores(core, t_own[:, cols], t_other[:, cols], tbuf.at[i])
        v = vf[:, cols]
        phikb = phik_ref[:, cols].astype(BF16)
        state, norm = get_state(pre, i)
        stateb = state.astype(BF16)
        phiq = feature_map(q, w_ref[i])
        phiqb = phiq.astype(BF16)
        scores = jnp.where(mask, dot(phiqb, phikb, ((1,), (1,))), 0.0)
        num = dot(scores.astype(BF16), v, ((1,), (0,))) + dot(phiqb, stateb, ((1,), (0,)))
        den = jnp.sum(
            scores[:, :WIDTH] + scores[:, WIDTH:] + phiq * norm, axis=1, keepdims=True
        )
        inv = 1.0 / den
        y = num * inv
        ybuf[i] = y
        y_own[:, cols] = ybuf[i, mine, :].astype(BF16)
        y_send[:, cols] = ybuf[i, theirs, :]
        err = y - t.astype(F32)
        loss_ref[...] += jnp.sum((err * err).reshape(TOK // 8, 8, WIDTH), axis=0)
        g = scale * err
        dnumb = (g * inv).astype(BF16)
        dden = -jnp.sum(g * y, axis=1, keepdims=True) * inv
        rev = dot(phiqb, dnumb, ((0,), (0,)))
        put_state(send, i, rev, jnp.sum(phiq * dden, axis=0, keepdims=True))
        grid = jnp.where(mask, dot(dnumb, v, ((1,), (1,))) + dden, 0.0)
        gridb = grid.astype(BF16)
        dphiq = dot(gridb, phikb, ((1,), (0,))) + dot(dnumb, stateb, ((1,), (1,)))
        dphiq = dphiq + dden * norm
        dphik_ref[:, cols] = dot(gridb, phiqb, ((0,), (0,)))
        grad_ref[64 * i : 64 * (i + 1), :] = soft_back(phiq, dphiq, q)


def final_kernel(kf, vf, phik_ref, dphik_ref, suf, grad_ref, loss_ref, send):
    row = jnp.sum(loss_ref[...], axis=0, keepdims=True)
    for i in range(GRP):
        cols = slice(WIDTH * i, WIDTH * (i + 1))
        state, norm = get_state(suf, i)
        dphik = dphik_ref[:, cols] + dot(vf[:, cols], state.astype(BF16), ((1,), (1,))) + norm
        grad_key = soft_back(phik_ref[:, cols], dphik, kf[:, cols])
        both = jnp.concatenate([grad_ref[64 * i : 64 * (i + 1), :], grad_key], axis=0)
        put_state(send, i, both, row)


SCAN_STEPS = 4
SCAN_PIECES = NCHIP // SCAN_STEPS
SCAN_ROWS = SCAN_PIECES * PIECE


def scan_kernel(x_ref, o_ref, acc_ref, *, reverse):
    @pl.when(pl.program_id(0) == 0)
    def _():
        acc_ref[...] = jnp.zeros_like(acc_ref)

    acc = acc_ref[...]
    order = range(SCAN_PIECES)
    for j in reversed(order) if reverse else order:
        o_ref[PIECE * j : PIECE * (j + 1), :] = acc
        acc = acc + x_ref[PIECE * j : PIECE * (j + 1), :]
    acc_ref[...] = acc


def sum_kernel(x_ref, o_ref):
    acc = x_ref[0:PIECE, :]
    for j in range(1, NCHIP):
        acc = acc + x_ref[PIECE * j : PIECE * (j + 1), :]
    for j in range(NCHIP):
        o_ref[PIECE * j : PIECE * (j + 1), :] = acc


def unpack_kernel(core_ref, mine, theirs, gq, gk, loss_ref):
    core = core_ref[0]
    half = pl.program_id(0)
    total = jnp.sum(mine[32:33, :] + theirs[32:33, :], keepdims=True)
    loss_ref[...] = total.reshape(1, 1) * (1.0 / (HEADS * WIDTH) / (NCHIP * TOK))

    def put(src):
        for i in range(HALF):
            for q in range(4):
                at = (4 * i + q) * PIECE
                dst = gq if q < 2 else gk
                dst[i, 32 * (q % 2) : 32 * (q % 2) + 32, :] = src[at : at + 32, :]

    @pl.when(half == core)
    def _():
        put(mine)

    @pl.when(half != core)
    def _():
        put(theirs)


def merge_kernel(core_ref, own, other, out):
    core = core_ref[0]

    @pl.when(pl.program_id(0) == core)
    def _():
        out[...] = own[...]

    @pl.when(pl.program_id(0) != core)
    def _():
        out[...] = other[...].astype(BF16)


def call(body, core, args, in_specs, outs, out_specs, scratch=(), steps=STEPS, name=None):
    spec = pltpu.PrefetchScalarGridSpec(
        num_scalar_prefetch=0 if core is None else 1,
        grid=(steps,),
        in_specs=in_specs,
        out_specs=out_specs,
        scratch_shapes=list(scratch),
    )
    lead = () if core is None else (core,)
    return pl.pallas_call(body, grid_spec=spec, out_shape=outs, name=name)(*lead, *args)


def sds(shape, dtype=F32):
    return jax.ShapeDtypeStruct(shape, dtype)


def exchange(x):
    pieces = lax.all_to_all(x.reshape(NCHIP, 1, PIECE * WIDTH), CHIPS, 0, 0, tiled=True)
    return pieces.reshape(ALL_ROWS, WIDTH)


def scan(x, reverse):
    at = (lambda g: (SCAN_STEPS - 1 - g, 0)) if reverse else (lambda g: (g, 0))
    spec = pl.BlockSpec((SCAN_ROWS, WIDTH), at)
    return call(
        functools.partial(scan_kernel, reverse=reverse),
        None, (x,), [spec], sds((ALL_ROWS, WIDTH)), spec,
        [pltpu.VMEM((PIECE, WIDTH), F32)], SCAN_STEPS, "scan",
    )


def swap(x):
    return lax.ppermute(x, "c", [(0, 1), (1, 0)])


def shards(queries, keys, values, teacher, query_map, key_map):
    c = lax.axis_index("c").astype(jnp.int32)
    core = c.reshape(1)
    half = HALF * WIDTH
    gcols = GRP * WIDTH

    def others(x):
        part = lax.dynamic_slice(x, (0, (1 - c) * half), (ROWS, half))
        return swap(part.astype(F32))

    k_other, v_other = others(keys), others(values)
    q_other, t_other = others(queries), others(teacher)

    own = pl.BlockSpec((ROWS, gcols), lambda g, c: (0, c[0] * STEPS + g))
    other = pl.BlockSpec((ROWS, gcols), lambda g, c: (0, g))
    weight = pl.BlockSpec((GRP, 64, WIDTH), lambda g, c: (c[0] * STEPS + g, 0, 0))
    full = pl.BlockSpec((TOK, gcols), lambda g, *c: (0, g))
    pieces = pl.BlockSpec((GROWS, WIDTH), lambda g, *c: (g, 0))
    grads = pl.BlockSpec((GRP * 64, WIDTH), lambda g, *c: (g, 0))
    lossy = pl.BlockSpec((8, WIDTH), lambda g, *c: (0, 0))
    payload = sds((ALL_ROWS, WIDTH))
    buf = pltpu.VMEM((GRP, TOK, WIDTH), BF16)

    kf, vf, phik, send = call(
        key_kernel, core, (keys, k_other, values, v_other, key_map),
        [own, other, own, other, weight],
        (sds((TOK, half), BF16), sds((TOK, half), BF16), sds((TOK, half)), payload),
        (full, full, full, pieces), [buf, buf], name="keys",
    )
    pre = exchange(scan(exchange(send), False))
    y_own, y_send, send, dphik, grad_query, loss = call(
        query_kernel, core,
        (queries, q_other, teacher, t_other, query_map, phik, vf, pre),
        [own, other, own, other, weight, full, full, pieces],
        (
            sds((ROWS, half), BF16), sds((ROWS, half)), payload, sds((TOK, half)),
            sds((HALF * 64, WIDTH)), sds((8, WIDTH)),
        ),
        (other, other, pieces, full, grads, lossy),
        [buf, buf, pltpu.VMEM((GRP, TOK, WIDTH), F32)], name="queries",
    )
    y_other = swap(y_send)
    suf = exchange(scan(exchange(send), True))
    send = call(
        final_kernel, None, (kf, vf, phik, dphik, suf, grad_query, loss),
        [full, full, full, full, pieces, grads, lossy], payload, pieces, name="final",
    )
    whole = pl.BlockSpec((ALL_ROWS, WIDTH), lambda g, *c: (0, 0))
    spread = call(
        sum_kernel, None, (exchange(send),), [whole], payload, whole, steps=1, name="sum"
    )
    mine = exchange(spread)
    theirs = swap(mine)
    gmap = pl.BlockSpec((HALF, 64, WIDTH), lambda g, c: (g, 0, 0))
    grad_query, grad_key, loss = call(
        unpack_kernel, core, (mine, theirs), [whole, whole],
        (sds((HEADS, 64, WIDTH)), sds((HEADS, 64, WIDTH)), sds((1, 1))),
        (gmap, gmap, pl.BlockSpec((1, 1), lambda g, c: (0, 0))), steps=2, name="unpack",
    )
    wide = pl.BlockSpec((ROWS, half), lambda g, c: (0, 0))
    attn = call(
        merge_kernel, core, (y_own, y_other), [wide, wide],
        sds((ROWS, HEADS * WIDTH), BF16),
        pl.BlockSpec((ROWS, half), lambda g, c: (0, g)), steps=2, name="merge",
    )
    return attn, loss[0, 0], grad_query, grad_key


def solution(mesh):
    fine = Mesh(mesh.devices.reshape(4, 4, 4, 2), ("x", "z", "y", "c"))
    tokens = P(("x", "z", "y", "c"), None)
    return jax.shard_map(
        shards,
        mesh=fine,
        in_specs=(tokens, tokens, tokens, tokens, P(), P()),
        out_specs=(tokens, P(), P(), P()),
        check_vma=False,
    )
```

```python
import functools

import jax
import jax.numpy as jnp
from jax import lax
from jax.experimental import pallas as pl
from jax.experimental.pallas import tpu as pltpu
from jax.sharding import Mesh
from jax.sharding import PartitionSpec as P

F32 = jnp.float32
BF16 = jnp.bfloat16
CHIPS = ("x", "z", "y")
NCHIP = 64
HEADS = 32
HALF = 16
ROWS = 128
TOK = 256
WIDTH = 128
PIECE = 33
PAIRS = HALF // 2
PROWS = 2 * 4 * PIECE

NN = ((1,), (0,))
NT = ((1,), (1,))


def dot(a, b, dims=NN):
    return lax.dot_general(a, b, (dims, ((), ())), preferred_element_type=F32)


def two_parts(x):
    high = x.astype(BF16)
    return high, (x - high.astype(F32)).astype(BF16)


def feature_map(x, w):
    logits = dot(w, x, NT)
    e_one = jnp.exp(logits - jnp.max(logits, axis=0, keepdims=True))
    e_two = jnp.exp(jnp.min(logits, axis=0, keepdims=True) - logits)
    one = e_one * (1.0 / jnp.sum(e_one, axis=0, keepdims=True))
    two = e_two * (1.0 / jnp.sum(e_two, axis=0, keepdims=True))
    return jnp.concatenate([one, two], axis=0)


def soft_back(phi, dphi, x):
    prod = phi * dphi
    one = prod[:64] - phi[:64] * jnp.sum(prod[:64], axis=0, keepdims=True)
    two = prod[64:] - phi[64:] * jnp.sum(prod[64:], axis=0, keepdims=True)
    return dot((one - two).astype(BF16), x)


def columns(h, core=None):
    at = h if core is None else core * HALF + h
    return pl.ds(pl.multiple_of(at * WIDTH, WIDTH), WIDTH)


def both_cores(own, other, h, core):
    return jnp.concatenate(
        [own[:, columns(h, core)], other[:, columns(h)].astype(BF16)], axis=0
    )


def put_state(ref, pair, i, state, row):
    for q in range(4):
        at = (4 * i + q) * PIECE
        ref[pair, at : at + 32, :] = state[32 * q : 32 * q + 32]
        ref[pair, at + 32 : at + 33, :] = row


def get_state(ref, pair, i):
    parts = [ref[pair, (4 * i + q) * PIECE : (4 * i + q) * PIECE + 32, :] for q in range(4)]
    at = 4 * i * PIECE + 32
    return jnp.concatenate(parts, axis=0), ref[pair, at : at + 1, :]


def unit():
    shape = (WIDTH, WIDTH)
    same = lax.broadcasted_iota(jnp.int32, shape, 0) == lax.broadcasted_iota(jnp.int32, shape, 1)
    return same.astype(F32).astype(BF16)


def down_rows(row, lanes, eye):
    high, low = two_parts(jnp.broadcast_to(row, (lanes, WIDTH)))
    return dot(jnp.concatenate([eye, eye], axis=1), jnp.concatenate([high, low], axis=1), NT)


def causal(core):
    shift = core * ROWS
    at_query = lax.broadcasted_iota(jnp.int32, (TOK, TOK), 0) ^ shift
    at_key = lax.broadcasted_iota(jnp.int32, (TOK, TOK), 1) ^ shift
    return at_query >= at_key


def over_heads(body):
    def pair(p, carry):
        for i in range(2):
            body(p, i, 2 * p + i)
        return carry

    lax.fori_loop(0, PAIRS, pair, 0)


def key_kernel(core_ref, k_own, k_other, v_own, v_other, w_ref, kf, vf, phik_ref, send):
    core = core_ref[0]
    ones = jnp.ones((8, TOK), BF16)

    def head(p, i, h):
        k = both_cores(k_own, k_other, h, core)
        v = both_cores(v_own, v_other, h, core)
        kf[h] = k
        vf[h] = v
        phik = feature_map(k, w_ref[core * HALF + h])
        phik_ref[h] = phik
        phikb = phik.astype(BF16)
        put_state(send, p, i, dot(phikb, v), dot(ones, phikb, NT)[:1])

    over_heads(head)


def score_kernel(core_ref, q_own, q_other, w_ref, phik_ref, vf, qf, phiq_ref, phiqb_ref, part):
    core = core_ref[0]
    mask = causal(core)
    ones = jnp.ones((TOK, WIDTH), BF16)

    def head(p, i, h):
        q = both_cores(q_own, q_other, h, core)
        qf[h] = q
        phiq = feature_map(q, w_ref[core * HALF + h])
        phiq_ref[h] = phiq
        phiqb = phiq.astype(BF16).T
        phiqb_ref[h] = phiqb
        scores = jnp.where(mask, dot(phiqb, phik_ref[h].astype(BF16)), 0.0)
        part[h] = dot(scores.astype(BF16), jnp.concatenate([vf[h], ones], axis=1))

    over_heads(head)


def out_kernel(
    core_ref, pre, phiq_ref, phiqb_ref, part, t_own, t_other,
    y_own, y_send, dd, dden_ref, send, loss_ref,
):
    core = core_ref[0]
    eye = unit()
    ones = jnp.ones((8, TOK), BF16)
    none = jnp.zeros((WIDTH, WIDTH), BF16)
    scale = 2.0 / (HEADS * WIDTH)
    loss_ref[...] = jnp.zeros_like(loss_ref)

    def head(p, i, h):
        state, norm = get_state(pre, p, i)
        high, low = two_parts(down_rows(norm, WIDTH, eye))
        right = jnp.concatenate(
            [
                jnp.concatenate([state.astype(BF16), high], axis=1),
                jnp.concatenate([none, low], axis=1),
            ],
            axis=0,
        )
        phiqb = phiqb_ref[h]
        both = part[h] + dot(jnp.concatenate([phiqb, phiqb], axis=1), right)
        inv = 1.0 / both[:, WIDTH:]
        y = both[:, :WIDTH] * inv
        y_own[:, columns(h)] = y[:ROWS].astype(BF16)
        y_send[:, columns(h)] = y[ROWS:]
        t = both_cores(t_own, t_other, h, core)
        err = y - t.astype(F32)
        loss_ref[...] += jnp.sum((err * err).reshape(TOK // 8, 8, WIDTH), axis=0)
        dnum = (scale * err) * inv
        dnumb = dnum.astype(BF16)
        high, low = two_parts(dnum * y)
        dd[h] = jnp.concatenate([dnumb, high], axis=1)
        dden = -dot(ones, jnp.concatenate([high, low], axis=1), NT)
        dden_ref[h] = dden
        phiqt = phiq_ref[h].astype(BF16)
        high, low = two_parts(dden)
        rnorm = dot(high, phiqt, NT) + dot(low, phiqt, NT)
        put_state(send, p, i, dot(phiqt, dnumb), rnorm[:1])

    over_heads(head)


def grid_kernel(
    core_ref, pre, dd, dden_ref, phik_ref, phiq_ref, vf, qf, dphik_ref, grad_ref,
):
    mask = causal(core_ref[0])
    eye = unit()
    minus = jnp.full((TOK, WIDTH), -1.0, BF16)

    def head(p, i, h):
        state, norm = get_state(pre, p, i)
        both = dd[h]
        grid = dot(both, jnp.concatenate([vf[h], minus], axis=1), NT)
        gridb = jnp.where(mask, grid, 0.0).astype(BF16)
        phiq = phiq_ref[h]
        dphik_ref[h] = dot(phiq.astype(BF16), gridb)
        dphiq = dot(phik_ref[h].astype(BF16), gridb, NT)
        dphiq = dphiq + dot(state.astype(BF16), both[:, :WIDTH], NT)
        dphiq = dphiq + down_rows(norm, TOK, eye) * dden_ref[h][:1]
        grad_ref[h] = soft_back(phiq, dphiq, qf[h])

    over_heads(head)


def last_kernel(suf, vf, kf, phik_ref, dphik_ref, grad_ref, loss_ref, send):
    row = jnp.sum(loss_ref[...], axis=0, keepdims=True)
    eye = unit()

    def head(p, i, h):
        state, norm = get_state(suf, p, i)
        dphik = dphik_ref[h] + dot(state.astype(BF16), vf[h], NT) + down_rows(norm, TOK, eye)
        grad_key = soft_back(phik_ref[h], dphik, kf[h])
        put_state(send, p, i, jnp.concatenate([grad_ref[h], grad_key], axis=0), row)

    over_heads(head)


def scan_kernel(x_ref, o_ref, *, reverse):
    def pieces(step, acc):
        block = PAIRS - 1 - step if reverse else step
        order = range(8)
        for j in reversed(order) if reverse else order:
            o_ref[block, PIECE * j : PIECE * (j + 1), :] = acc
            acc = acc + x_ref[block, PIECE * j : PIECE * (j + 1), :]
        return acc

    lax.fori_loop(0, PAIRS, pieces, jnp.zeros((PIECE, WIDTH), F32))


def sum_kernel(x_ref, o_ref):
    def add(block, acc):
        for j in range(8):
            acc = acc + x_ref[block, PIECE * j : PIECE * (j + 1), :]
        return acc

    acc = lax.fori_loop(0, PAIRS, add, jnp.zeros((PIECE, WIDTH), F32))

    def put(block, carry):
        for j in range(8):
            o_ref[block, PIECE * j : PIECE * (j + 1), :] = acc
        return carry

    lax.fori_loop(0, PAIRS, put, 0)


def unpack_kernel(core_ref, mine, theirs, gq, gk, loss_ref):
    core = core_ref[0]
    total = jnp.sum(mine[0, 32:33, :] + theirs[0, 32:33, :], keepdims=True)
    loss_ref[...] = total.reshape(1, 1) * (1.0 / (HEADS * WIDTH) / (NCHIP * TOK))
    for src, start in ((mine, core * HALF), (theirs, (1 - core) * HALF)):

        def pair(p, carry, src=src, start=start):
            for i in range(2):
                for q in range(4):
                    at = (4 * i + q) * PIECE
                    dst = gq if q < 2 else gk
                    rows = slice(32 * (q % 2), 32 * (q % 2) + 32)
                    dst[start + 2 * p + i, rows, :] = src[p, at : at + 32, :]
            return carry

        lax.fori_loop(0, PAIRS, pair, 0)


def merge_kernel(core_ref, own, other, out):
    core = core_ref[0]

    def head(h, carry):
        out[:, columns(h, core)] = own[:, columns(h)]
        out[:, columns(h, 1 - core)] = other[:, columns(h)].astype(BF16)
        return carry

    lax.fori_loop(0, HALF, head, 0)


def call(body, name, args, outs, scalar=True):
    vmem = pl.BlockSpec(memory_space=pltpu.VMEM)
    specs = [vmem] * len(args)
    if scalar:
        specs[0] = pl.BlockSpec(memory_space=pltpu.SMEM)
    many = isinstance(outs, tuple)
    return pl.pallas_call(
        body,
        in_specs=specs,
        out_specs=(vmem,) * len(outs) if many else vmem,
        out_shape=outs,
        name=name,
        compiler_params=pltpu.CompilerParams(vmem_limit_bytes=56 * 1024 * 1024),
    )(*args)


def sds(shape, dtype=F32):
    return jax.ShapeDtypeStruct(shape, dtype)


PAYLOAD = sds((PAIRS, PROWS, WIDTH))


def exchange(x):
    pieces = lax.all_to_all(x.reshape(NCHIP, 1, PIECE * WIDTH), CHIPS, 0, 0, tiled=True)
    return pieces.reshape(PAIRS, PROWS, WIDTH)


def scan(x, reverse):
    return call(functools.partial(scan_kernel, reverse=reverse), "scan", (x,), PAYLOAD, False)


def swap(x):
    return lax.ppermute(x, "c", [(0, 1), (1, 0)])


def shards(queries, keys, values, teacher, query_map, key_map):
    c = lax.axis_index("c").astype(jnp.int32)
    core = c.reshape(1)
    half = HALF * WIDTH

    def others(x):
        part = lax.dynamic_slice(x, (0, (1 - c) * half), (ROWS, half))
        return swap(part.astype(F32))

    k_other, v_other = others(keys), others(values)
    q_other, t_other = others(queries), others(teacher)

    natural = sds((HALF, TOK, WIDTH), BF16)
    features = sds((HALF, WIDTH, TOK))
    wide = sds((HALF, TOK, 2 * WIDTH))

    kf, vf, phik, send = call(
        key_kernel, "keys", (core, keys, k_other, values, v_other, key_map),
        (natural, natural, features, PAYLOAD),
    )
    gathered = exchange(send)
    qf, phiq, phiqb, part = call(
        score_kernel, "scores", (core, queries, q_other, query_map, phik, vf),
        (natural, features, natural, wide),
    )
    pre = exchange(scan(gathered, False))
    y_own, y_send, dd, dden, send, loss = call(
        out_kernel, "outs", (core, pre, phiq, phiqb, part, teacher, t_other),
        (
            sds((ROWS, half), BF16), sds((ROWS, half)), sds((HALF, TOK, 2 * WIDTH), BF16),
            sds((HALF, 8, TOK)), PAYLOAD, sds((8, WIDTH)),
        ),
    )
    y_other = swap(y_send)
    gathered = exchange(send)
    dphik, grad_query = call(
        grid_kernel, "grids", (core, pre, dd, dden, phik, phiq, vf, qf),
        (features, sds((HALF, 64, WIDTH))),
    )
    suf = exchange(scan(gathered, True))
    attn = call(
        merge_kernel, "merge", (core, y_own, y_other), sds((ROWS, HEADS * WIDTH), BF16)
    )
    send = call(
        last_kernel, "last", (suf, vf, kf, phik, dphik, grad_query, loss), PAYLOAD, False
    )
    mine = exchange(call(sum_kernel, "sum", (exchange(send),), PAYLOAD, False))
    theirs = swap(mine)
    grad = sds((HEADS, 64, WIDTH))
    grad_query, grad_key, loss = call(
        unpack_kernel, "unpack", (core, mine, theirs), (grad, grad, sds((1, 1)))
    )
    return attn, loss[0, 0], grad_query, grad_key


def solution(mesh):
    fine = Mesh(mesh.devices.reshape(4, 4, 4, 2), ("x", "z", "y", "c"))
    tokens = P(("x", "z", "y", "c"), None)
    return jax.shard_map(
        shards,
        mesh=fine,
        in_specs=(tokens, tokens, tokens, tokens, P(), P()),
        out_specs=(tokens, P(), P(), P()),
        check_vma=False,
    )
```

```python
import functools

import jax
import jax.numpy as jnp
from jax import lax
from jax.experimental import pallas as pl
from jax.experimental.pallas import tpu as pltpu
from jax.sharding import Mesh
from jax.sharding import PartitionSpec as P

F32 = jnp.float32
BF16 = jnp.bfloat16
CHIPS = ("x", "z", "y")
NCHIP = 64
HEADS = 32
HALF = 16
ROWS = 128
TOK = 256
WIDTH = 128
PIECE = 33
PAIRS = HALF // 2
GRP = 4
STEPS = HALF // GRP
PROWS = 2 * 4 * PIECE

NN = ((1,), (0,))
NT = ((1,), (1,))


def dot(a, b, dims=NN):
    return lax.dot_general(a, b, (dims, ((), ())), preferred_element_type=F32)


def two_parts(x):
    high = x.astype(BF16)
    return high, (x - high.astype(F32)).astype(BF16)


def soft_maps(logits):
    e_one = jnp.exp(logits - jnp.max(logits, axis=0, keepdims=True))
    e_two = jnp.exp(jnp.min(logits, axis=0, keepdims=True) - logits)
    one = e_one * (1.0 / jnp.sum(e_one, axis=0, keepdims=True))
    two = e_two * (1.0 / jnp.sum(e_two, axis=0, keepdims=True))
    return jnp.concatenate([one, two], axis=0)


def soft_back(phi, dphi, x):
    prod = phi * dphi
    one = prod[:64] - phi[:64] * jnp.sum(prod[:64], axis=0, keepdims=True)
    two = prod[64:] - phi[64:] * jnp.sum(prod[64:], axis=0, keepdims=True)
    return dot((one - two).astype(BF16), x)


def columns(h):
    return pl.ds(pl.multiple_of(h * WIDTH, WIDTH), WIDTH)


def both_cores(own, other, h, base=0):
    return jnp.concatenate(
        [own[:, columns(h)], other[:, columns(base + h)].astype(BF16)], axis=0
    )


def put_state(ref, pair, i, state, row):
    for q in range(4):
        at = (4 * i + q) * PIECE
        ref[pair, at : at + 32, :] = state[32 * q : 32 * q + 32]
        ref[pair, at + 32 : at + 33, :] = row


def get_state(ref, pair, i):
    parts = [ref[pair, (4 * i + q) * PIECE : (4 * i + q) * PIECE + 32, :] for q in range(4)]
    at = 4 * i * PIECE + 32
    return jnp.concatenate(parts, axis=0), ref[pair, at : at + 1, :]


def unit():
    shape = (WIDTH, WIDTH)
    same = lax.broadcasted_iota(jnp.int32, shape, 0) == lax.broadcasted_iota(jnp.int32, shape, 1)
    return same.astype(F32).astype(BF16)


def down_rows(row, lanes, eye):
    high, low = two_parts(jnp.broadcast_to(row, (lanes, WIDTH)))
    return dot(jnp.concatenate([eye, eye], axis=1), jnp.concatenate([high, low], axis=1), NT)


def causal(core):
    shift = core * ROWS
    at_query = lax.broadcasted_iota(jnp.int32, (TOK, TOK), 0) ^ shift
    at_key = lax.broadcasted_iota(jnp.int32, (TOK, TOK), 1) ^ shift
    return at_query >= at_key


def over_heads(body):
    running = []
    waiting = list(range(GRP))
    while running or waiting:
        if waiting:
            h = waiting.pop(0)
            running.append(body(h // 2, h % 2, h))
        running = [r for r in running if next(r, "end") != "end"]


def key_kernel(core_ref, k_own, k_other, v_own, v_other, w_ref, kf, vf, phik_ref, send):
    ones = jnp.ones((8, TOK), BF16)
    base = pl.program_id(0) * GRP

    def head(p, i, h):
        k = both_cores(k_own, k_other, h, base)
        kf[h] = k
        logits = dot(w_ref[h], k, NT)
        yield
        phik = soft_maps(logits)
        phik_ref[h] = phik
        phikb = phik.astype(BF16)
        v = both_cores(v_own, v_other, h, base)
        vf[h] = v
        yield
        state = dot(phikb, v)
        row = dot(ones, phikb, NT)[:1]
        yield
        put_state(send, p, i, state, row)

    over_heads(head)


def score_kernel(
    core_ref, q_own, q_other, w_ref, phik_ref, vf, qf, phiq_ref, phiqt_ref, phiqb_ref, part
):
    mask = causal(core_ref[0])
    ones = jnp.ones((TOK, WIDTH), BF16)

    def head(p, i, h):
        q = both_cores(q_own, q_other, h)
        qf[h] = q
        logits = dot(w_ref[h], q, NT)
        yield
        phiq = soft_maps(logits)
        phiq_ref[h] = phiq
        phiqt = phiq.astype(BF16)
        phiqt_ref[h] = phiqt
        phiqb = phiqt.T
        phiqb_ref[h] = phiqb
        yield
        scores = dot(phiqb, phik_ref[h].astype(BF16))
        yield
        scoresb = jnp.where(mask, scores, 0.0).astype(BF16)
        part[h] = dot(scoresb, jnp.concatenate([vf[h], ones], axis=1))

    over_heads(head)


def out_kernel(
    core_ref, pre, phiqt_ref, phiqb_ref, part, t_own, t_other,
    y_own, y_send, dd, dden_ref, send, loss_ref,
):
    eye = unit()
    ones = jnp.ones((8, TOK), BF16)
    none = jnp.zeros((WIDTH, WIDTH), BF16)
    scale = 2.0 / (HEADS * WIDTH)
    first = pl.program_id(0) * (GRP // 2)

    @pl.when(pl.program_id(0) == 0)
    def _():
        loss_ref[...] = jnp.zeros_like(loss_ref)

    def head(p, i, h):
        state, norm = get_state(pre, first + p, i)
        down = down_rows(norm, WIDTH, eye)
        yield
        high, low = two_parts(down)
        right = jnp.concatenate(
            [
                jnp.concatenate([state.astype(BF16), high], axis=1),
                jnp.concatenate([none, low], axis=1),
            ],
            axis=0,
        )
        phiqb = phiqb_ref[h]
        carried = dot(jnp.concatenate([phiqb, phiqb], axis=1), right)
        yield
        both = part[h] + carried
        inv = 1.0 / both[:, WIDTH:]
        y = both[:, :WIDTH] * inv
        y_own[:, columns(h)] = y[:ROWS].astype(BF16)
        y_send[:, columns(h)] = y[ROWS:]
        err = y - both_cores(t_own, t_other, h).astype(F32)
        loss_ref[...] += jnp.sum((err * err).reshape(TOK // 8, 8, WIDTH), axis=0)
        dnum = (scale * err) * inv
        dnumb = dnum.astype(BF16)
        high, low = two_parts(dnum * y)
        both = jnp.concatenate([dnumb, high, low], axis=1)
        dd[h] = both
        yield
        dden = -dot(ones, both[:, WIDTH:], NT)
        rev = dot(phiqt_ref[h], dnumb)
        yield
        dden_ref[h] = dden
        high, low = two_parts(dden)
        phiqt = phiqt_ref[h]
        rnorm = dot(high, phiqt, NT) + dot(low, phiqt, NT)
        yield
        put_state(send, p, i, rev, rnorm[:1])

    over_heads(head)


def grid_kernel(
    core_ref, pre, dd, dden_ref, phik_ref, phiq_ref, phiqt_ref, vf, qf, dphik_ref, grad_ref,
):
    mask = causal(core_ref[0])
    eye = unit()
    minus = jnp.full((TOK, WIDTH), -1.0, BF16)

    def head(p, i, h):
        state, norm = get_state(pre, p, i)
        grid = dot(dd[h], jnp.concatenate([vf[h], minus, minus], axis=1), NT)
        yield
        gridb = jnp.where(mask, grid, 0.0).astype(BF16)
        dphik_ref[h] = dot(phiqt_ref[h], gridb)
        left = jnp.concatenate([phik_ref[h].astype(BF16), state.astype(BF16)], axis=1)
        dphiq = dot(left, jnp.concatenate([gridb, dd[h, :, :WIDTH]], axis=1), NT)
        down = down_rows(norm, TOK, eye)
        yield
        grad_ref[h] = soft_back(phiq_ref[h], dphiq + down * dden_ref[h][:1], qf[h])

    over_heads(head)


def merge_kernel(core_ref, y_own, y_other, attn):
    core = core_ref[0]
    wide = GRP * WIDTH
    at = pl.program_id(0) * wide
    mine = pl.multiple_of(core * HALF * WIDTH + at, wide)
    theirs = pl.multiple_of((1 - core) * HALF * WIDTH + at, wide)
    attn[:, pl.ds(mine, wide)] = y_own[...]
    attn[:, pl.ds(theirs, wide)] = y_other[...].astype(BF16)


def last_kernel(core_ref, suf, vf, kf, phik_ref, dphik_ref, grad_ref, loss_ref, send):
    row = jnp.sum(loss_ref[...], axis=0, keepdims=True)
    eye = unit()
    first = pl.program_id(0) * (GRP // 2)

    def head(p, i, h):
        state, norm = get_state(suf, first + p, i)
        carried = dot(state.astype(BF16), vf[h], NT) + down_rows(norm, TOK, eye)
        yield
        grad_key = soft_back(phik_ref[h], dphik_ref[h] + carried, kf[h])
        yield
        put_state(send, p, i, jnp.concatenate([grad_ref[h], grad_key], axis=0), row)

    over_heads(head)


BLOCKS = PAIRS // STEPS


def scan_kernel(core_ref, x_ref, o_ref, acc_ref, *, reverse):
    step = pl.program_id(0)

    @pl.when(step == 0)
    def _():
        acc_ref[...] = jnp.zeros_like(acc_ref)

    first = (STEPS - 1 - step if reverse else step) * BLOCKS
    order = [(b, j) for b in range(BLOCKS) for j in range(8)]
    acc = acc_ref[...]
    for b, j in reversed(order) if reverse else order:
        o_ref[b, PIECE * j : PIECE * (j + 1), :] = acc
        acc = acc + x_ref[first + b, PIECE * j : PIECE * (j + 1), :]
    acc_ref[...] = acc


def sum_kernel(core_ref, x_ref, o_ref, acc_ref):
    @pl.when(pl.program_id(0) == 0)
    def _():
        acc = x_ref[0, :PIECE, :]
        for n in range(1, NCHIP):
            j = n % 8
            acc = acc + x_ref[n // 8, PIECE * j : PIECE * (j + 1), :]
        acc_ref[...] = acc

    acc = acc_ref[...]
    for b in range(BLOCKS):
        for j in range(8):
            o_ref[b, PIECE * j : PIECE * (j + 1), :] = acc


def unpack_kernel(core_ref, mine, theirs, gq, gk, loss_ref):
    step = pl.program_id(0)
    total = jnp.sum(mine[0, 32:33, :] + theirs[0, 32:33, :], keepdims=True)
    loss_ref[...] = total.reshape(1, 1) * (1.0 / (HEADS * WIDTH) / (NCHIP * TOK))
    first = lax.rem(step, 2) * (PAIRS // 2)

    def put(src):
        for p in range(PAIRS // 2):
            for i in range(2):
                for q in range(4):
                    at = (4 * i + q) * PIECE
                    dst = gq if q < 2 else gk
                    rows = slice(32 * (q % 2), 32 * (q % 2) + 32)
                    dst[2 * p + i, rows, :] = src[first + p, at : at + 32, :]

    @pl.when(step // 2 == core_ref[0])
    def _():
        put(mine)

    @pl.when(step // 2 != core_ref[0])
    def _():
        put(theirs)


def call(body, name, core, args, outs, scratch=()):
    specs, values = [], []
    for value, spec in args:
        space = pltpu.HBM
        if spec is None:
            spec = pl.BlockSpec(memory_space=pltpu.VMEM)
            space = pltpu.VMEM
        specs.append(spec)
        values.append(pltpu.with_memory_space_constraint(value, space))
    grid = pltpu.PrefetchScalarGridSpec(
        num_scalar_prefetch=1,
        grid=(STEPS,),
        in_specs=specs,
        out_specs=tuple(spec for _, spec in outs),
        scratch_shapes=list(scratch),
    )
    return pl.pallas_call(
        body,
        grid_spec=grid,
        out_shape=tuple(shape for shape, _ in outs),
        name=name,
        compiler_params=pltpu.CompilerParams(vmem_limit_bytes=48 * 1024 * 1024),
    )(core, *values)


def sds(shape, dtype=F32):
    return pltpu.HBM(shape, dtype)


def heads_block(*tail):
    return pl.BlockSpec((GRP,) + tail, lambda g, c: (g,) + (0,) * len(tail))


PAYLOAD = sds((PAIRS, PROWS, WIDTH))
PIECES = pl.BlockSpec((BLOCKS, PROWS, WIDTH), lambda g, c: (g, 0, 0))
ACC = pltpu.VMEM((PIECE, WIDTH), F32)


def exchange(x):
    pieces = lax.all_to_all(x.reshape(NCHIP, 1, PIECE * WIDTH), CHIPS, 0, 0, tiled=True)
    return pieces.reshape(PAIRS, PROWS, WIDTH)


def scan(core, x, reverse):
    at = (lambda g, c: (STEPS - 1 - g, 0, 0)) if reverse else (lambda g, c: (g, 0, 0))
    spec = pl.BlockSpec((BLOCKS, PROWS, WIDTH), at)
    return call(
        functools.partial(scan_kernel, reverse=reverse), "scan", core, [(x, None)],
        [(PAYLOAD, spec)], scratch=[ACC],
    )[0]


def swap(x):
    return lax.ppermute(x, "c", [(0, 1), (1, 0)])


def shards(queries, keys, values, teacher, query_map, key_map):
    c = lax.axis_index("c").astype(jnp.int32)
    half = HALF * WIDTH
    gcols = GRP * WIDTH

    def others(x):
        part = lax.dynamic_slice(x, (0, (1 - c) * half), (ROWS, half))
        return swap(part.astype(F32))

    k_other, v_other = others(keys), others(values)
    q_other, t_other = others(queries), others(teacher)

    core = c.reshape(1)
    own = pl.BlockSpec((ROWS, gcols), lambda g, c: (0, c[0] * STEPS + g))
    cols = pl.BlockSpec((ROWS, gcols), lambda g, c: (0, g))
    natural = (sds((HALF, TOK, WIDTH), BF16), heads_block(TOK, WIDTH))
    features = (sds((HALF, WIDTH, TOK)), heads_block(WIDTH, TOK))
    wide = (sds((HALF, TOK, 2 * WIDTH)), heads_block(TOK, 2 * WIDTH))
    triple = (sds((HALF, TOK, 3 * WIDTH), BF16), heads_block(TOK, 3 * WIDTH))
    halved = (sds((HALF, WIDTH, TOK), BF16), heads_block(WIDTH, TOK))
    row = (sds((HALF, 8, TOK)), heads_block(8, TOK))
    grads = (sds((HALF, 64, WIDTH)), heads_block(64, WIDTH))
    weight = pl.BlockSpec((GRP, 64, WIDTH), lambda g, c: (c[0] * STEPS + g, 0, 0))
    payload = (PAYLOAD, PIECES)
    lossy = (sds((8, WIDTH)), pl.BlockSpec((8, WIDTH), lambda g, c: (0, 0)))

    def with_spec(value, like):
        return (value, like[1])

    kf, vf, phik, send = call(
        key_kernel, "keys", core,
        [(keys, own), (k_other, None), (values, own), (v_other, None),
         (key_map, weight)],
        [natural, natural, features, payload],
    )
    gathered = exchange(send)
    qf, phiq, phiqt, phiqb, part = call(
        score_kernel, "scores", core,
        [(queries, own), (q_other, cols), (query_map, weight),
         with_spec(phik, features), with_spec(vf, natural)],
        [natural, features, halved, natural, wide],
    )
    pre = exchange(scan(core, gathered, False))
    y_own, y_send, dd, dden, send, loss = call(
        out_kernel, "outs", core,
        [(pre, None), with_spec(phiqt, halved), with_spec(phiqb, natural),
         with_spec(part, wide), (teacher, own), (t_other, cols)],
        [(sds((ROWS, half), BF16), cols), (sds((ROWS, half)), cols), triple, row, payload,
         lossy],
    )
    gathered = exchange(send)
    dphik, grad_query = call(
        grid_kernel, "grids", core,
        [(pre, PIECES), with_spec(dd, triple), with_spec(dden, row),
         with_spec(phik, features), with_spec(phiq, features), with_spec(phiqt, halved),
         with_spec(vf, natural), with_spec(qf, natural)],
        [features, grads],
    )
    gathered, dphik, grad_query, y_send = lax.optimization_barrier(
        (gathered, dphik, grad_query, y_send)
    )
    y_other = swap(y_send)
    attn, = call(
        merge_kernel, "merge", core, [(y_own, cols), (y_other, cols)],
        [(sds((ROWS, HEADS * WIDTH), BF16),
          pl.BlockSpec((ROWS, HEADS * WIDTH), lambda g, c: (0, 0)))],
    )
    suf = exchange(scan(core, gathered, True))
    suf, attn = lax.optimization_barrier((suf, attn))
    send, = call(
        last_kernel, "last", core,
        [(suf, None), with_spec(vf, natural), with_spec(kf, natural),
         with_spec(phik, features), with_spec(dphik, features),
         with_spec(grad_query, grads), with_spec(loss, lossy)],
        [payload],
    )
    spread, = call(sum_kernel, "sum", core, [(exchange(send), None)], [payload], scratch=[ACC])
    total = exchange(spread)
    grad = (sds((HEADS, 64, WIDTH)), pl.BlockSpec((HALF // 2, 64, WIDTH), lambda g, c: (g, 0, 0)))
    grad_query, grad_key, loss = call(
        unpack_kernel, "unpack", core, [(total, None), (swap(total), None)],
        [grad, grad, (sds((1, 1)), pl.BlockSpec((1, 1), lambda g, c: (0, 0)))],
    )
    return attn, loss[0, 0], grad_query, grad_key


def solution(mesh):
    fine = Mesh(mesh.devices.reshape(4, 4, 4, 2), ("x", "z", "y", "c"))
    tokens = P(("x", "z", "y", "c"), None)
    return jax.shard_map(
        shards,
        mesh=fine,
        in_specs=(tokens, tokens, tokens, tokens, P(), P()),
        out_specs=(tokens, P(), P(), P()),
        check_vma=False,
    )
```

```python
import functools

import jax
import jax.numpy as jnp
from jax import lax
from jax.experimental import pallas as pl
from jax.experimental.pallas import tpu as pltpu
from jax.sharding import Mesh
from jax.sharding import PartitionSpec as P

F32 = jnp.float32
BF16 = jnp.bfloat16
CHIPS = ("x", "z", "y")
NCHIP = 64
HEADS = 32
HALF = 16
ROWS = 128
TOK = 256
WIDTH = 128
PIECE = 33
PAIRS = HALF // 2
GROUPS = ((4, 12), (12, 4))
PROWS = 2 * 4 * PIECE

NN = ((1,), (0,))
NT = ((1,), (1,))


def dot(a, b, dims=NN):
    return lax.dot_general(a, b, (dims, ((), ())), preferred_element_type=F32)


def two_parts(x):
    high = x.astype(BF16)
    return high, (x - high.astype(F32)).astype(BF16)


def soft_maps(logits):
    e_one = jnp.exp(logits - jnp.max(logits, axis=0, keepdims=True))
    e_two = jnp.exp(jnp.min(logits, axis=0, keepdims=True) - logits)
    one = e_one * (1.0 / jnp.sum(e_one, axis=0, keepdims=True))
    two = e_two * (1.0 / jnp.sum(e_two, axis=0, keepdims=True))
    return jnp.concatenate([one, two], axis=0)


def soft_back(phi, dphi, x):
    prod = phi * dphi
    one = prod[:64] - phi[:64] * jnp.sum(prod[:64], axis=0, keepdims=True)
    two = prod[64:] - phi[64:] * jnp.sum(prod[64:], axis=0, keepdims=True)
    return dot((one - two).astype(BF16), x)


def columns(h):
    return slice(h * WIDTH, (h + 1) * WIDTH)


def both_cores(own, other, h):
    return jnp.concatenate(
        [own[:, columns(h)], other[:, columns(h)].astype(BF16)], axis=0
    )


def put_state(ref, h, state, row):
    pair = h // 2
    for q in range(4):
        at = (4 * (h % 2) + q) * PIECE
        ref[pair, at : at + 32, :] = state[32 * q : 32 * q + 32]
        ref[pair, at + 32 : at + 33, :] = row


def get_state(ref, h):
    first = 4 * (h % 2)
    parts = [ref[h // 2, (first + q) * PIECE : (first + q) * PIECE + 32, :] for q in range(4)]
    at = first * PIECE + 32
    return jnp.concatenate(parts, axis=0), ref[h // 2, at : at + 1, :]


def as_column(row, lanes):
    return jnp.broadcast_to(row, (lanes, row.shape[1])).T


def as_row(column):
    return jnp.broadcast_to(column, (column.shape[0], WIDTH)).T[:1]


def twice(x):
    return jnp.concatenate([x, x], axis=1)


def causal(core):
    shift = core * ROWS
    at_query = lax.broadcasted_iota(jnp.int32, (TOK, TOK), 0) ^ shift
    at_key = lax.broadcasted_iota(jnp.int32, (TOK, TOK), 1) ^ shift
    return at_query >= at_key


def key_kernel(core, k_own, k_other, v_own, v_other, w_ref, kf, vf, phik_ref, send):

    def head(h):
        k = both_cores(k_own, k_other, h)
        kf[h] = k
        logits = dot(w_ref[h], k, NT)
        yield
        phik = soft_maps(logits)
        phik_ref[h] = phik
        phikb = phik.astype(BF16)
        v = both_cores(v_own, v_other, h)
        vf[h] = v
        yield
        state = dot(phikb, v)
        yield
        put_state(send, h, state, as_row(jnp.sum(phik, axis=1, keepdims=True)))

    return head


def score_kernel(
    core, q_own, q_other, w_ref, phik_ref, vf, qf, phiq_ref, phiqb_ref, den_ref, num_ref
):
    mask = causal(core)
    ones = jnp.ones((8, 2 * TOK), BF16)

    def head(h):
        q = both_cores(q_own, q_other, h)
        qf[h] = q
        logits = dot(w_ref[h], q, NT)
        yield
        phiq = soft_maps(logits)
        phiq_ref[h] = phiq
        phiqb = phiq.astype(BF16).T
        phiqb_ref[h] = phiqb
        yield
        scores = dot(phiqb, phik_ref[h].astype(BF16))
        yield
        high, low = two_parts(jnp.where(mask, scores, 0.0))
        num_ref[h] = dot(high, vf[h])
        den_ref[h] = dot(ones, jnp.concatenate([high, low], axis=1), NT)

    return head


def out_kernel(
    core, pre, num_ref, phiq_ref, phiqb_ref, den_ref, t_own, t_other,
    y_own, y_send, dnum_ref, dden_ref, send, loss_ref,
):
    ones = jnp.ones((8, 2 * WIDTH), BF16)
    scale = 2.0 / (HEADS * WIDTH)
    loss_ref[...] = jnp.zeros_like(loss_ref)

    def head(h):
        state, norm = get_state(pre, h)
        carried = dot(phiqb_ref[h], state.astype(BF16))
        down = as_column(norm, WIDTH)
        yield
        phiq = phiq_ref[h]
        before = jnp.sum(phiq * twice(down), axis=0, keepdims=True)
        inv = as_column(1.0 / (den_ref[h][:1] + before), WIDTH)
        yield
        y = (num_ref[h] + carried) * inv
        y_own[:, columns(h)] = y[:ROWS].astype(BF16)
        y_send[:, columns(h)] = y[ROWS:]
        err = y - both_cores(t_own, t_other, h).astype(F32)
        loss_ref[...] += jnp.sum((err * err).reshape(TOK // 8, 8, WIDTH), axis=0)
        dnum = (scale * err) * inv
        dnumb = dnum.astype(BF16)
        dnum_ref[h] = dnumb
        high, low = two_parts(dnum * y)
        both = jnp.concatenate([high, low], axis=1)
        yield
        dden = -dot(ones, both, NT)
        rev = dot(phiq_ref[h].astype(BF16), dnumb)
        yield
        dden_ref[h] = dden
        rnorm = as_row(jnp.sum(phiq_ref[h] * dden[:1], axis=1, keepdims=True))
        yield
        put_state(send, h, rev, rnorm)

    return head


def out_kernel(
    core, pre, num_ref, phiqt_ref, phiqb_ref, den_ref, t_own, t_other,
    y_own, y_send, dnum_ref, dden_ref, send, loss_ref,
):
    ones = jnp.ones((8, 2 * WIDTH), BF16)
    none = jnp.zeros((WIDTH, WIDTH), BF16)
    scale = 2.0 / (HEADS * WIDTH)
    loss_ref[...] = jnp.zeros_like(loss_ref)

    def head(h):
        state, norm = get_state(pre, h)
        high, low = two_parts(as_column(norm, WIDTH))
        den = as_column(den_ref[h][:1], WIDTH)
        right = jnp.concatenate(
            [
                jnp.concatenate([state.astype(BF16), high], axis=1),
                jnp.concatenate([none, low], axis=1),
            ],
            axis=0,
        )
        yield
        both = dot(twice(phiqb_ref[h]), right)
        yield
        inv = 1.0 / (den + both[:, WIDTH:])
        y = (num_ref[h] + both[:, :WIDTH]) * inv
        y_own[:, columns(h)] = y[:ROWS].astype(BF16)
        y_send[:, columns(h)] = y[ROWS:]
        err = y - both_cores(t_own, t_other, h).astype(F32)
        loss_ref[...] += jnp.sum((err * err).reshape(TOK // 8, 8, WIDTH), axis=0)
        dnum = (scale * err) * inv
        dnumb = dnum.astype(BF16)
        dnum_ref[h] = dnumb
        high, low = two_parts(dnum * y)
        both = jnp.concatenate([high, low], axis=1)
        yield
        dden = -dot(ones, both, NT)
        rev = dot(phiqt_ref[h], dnumb)
        yield
        dden_ref[h] = dden
        high, low = two_parts(dden)
        phiqt = phiqt_ref[h]
        rnorm = dot(jnp.concatenate([high, low], axis=1), twice(phiqt), NT)
        yield
        put_state(send, h, rev, rnorm[:1])

    return head


def grid_kernel(
    core, dnum_ref, vf, dden_ref, phiq_ref, phik_ref, pre, qf, grad_ref, dphik_ref,
):
    mask = causal(core)

    def head(h):
        grid = dot(dnum_ref[h], vf[h], NT)
        column = as_column(dden_ref[h][:1], WIDTH)
        yield
        gridb = jnp.where(mask, grid + twice(column), 0.0).astype(BF16)
        dphik_ref[h] = dot(phiq_ref[h].astype(BF16), gridb)
        state, norm = get_state(pre, h)
        left = jnp.concatenate([phik_ref[h].astype(BF16), state.astype(BF16)], axis=1)
        dphiq = dot(left, jnp.concatenate([gridb, dnum_ref[h]], axis=1), NT)
        down = twice(as_column(norm, WIDTH))
        yield
        grad_ref[h] = soft_back(phiq_ref[h], dphiq + down * dden_ref[h][:1], qf[h])

    return head


def merge_kernel(core, y_own, y_other, attn_mine, attn_theirs):
    del core

    def head(h):
        attn_mine[:, columns(h)] = y_own[:, columns(h)]
        attn_theirs[:, columns(h)] = y_other[:, columns(h)].astype(BF16)
        yield

    return head


def last_kernel(
    core, suf, vf, phik_ref, kf, dphik_ref, grad_ref, loss_ref, loss_other, send
):
    row = jnp.sum(loss_ref[...] + loss_other[...], axis=0, keepdims=True)

    def head(h):
        state, norm = get_state(suf, h)
        carried = dot(state.astype(BF16), vf[h], NT) + twice(as_column(norm, WIDTH))
        yield
        grad_key = soft_back(phik_ref[h], dphik_ref[h] + carried, kf[h])
        yield
        put_state(send, h, jnp.concatenate([grad_ref[h], grad_key], axis=0), row)

    return head


def scan_kernel(core, x_ref, o_ref, *, reverse):
    del core
    acc = jnp.zeros((PIECE, WIDTH), F32)

    def head(h):
        nonlocal acc
        for j in range(3, -1, -1) if reverse else range(4):
            at = (4 * (h % 2) + j) * PIECE
            o_ref[h // 2, at : at + PIECE, :] = acc
            acc = acc + x_ref[h // 2, at : at + PIECE, :]
        yield

    return head


def sum_kernel(core_ref, x_ref, o_ref, buf, sems):
    del core_ref
    parts = []
    for b in range(PAIRS):
        part = x_ref[b, :PIECE, :]
        for j in range(1, 8):
            part = part + x_ref[b, PIECE * j : PIECE * (j + 1), :]
        parts.append(part)
    while len(parts) > 1:
        parts = [x + y for x, y in zip(parts[::2], parts[1::2])]
    for j in range(8):
        buf[PIECE * j : PIECE * (j + 1), :] = parts[0]
    copies = [pltpu.make_async_copy(buf, o_ref.at[b], sems.at[b]) for b in range(PAIRS)]
    for copy in copies:
        copy.start()
    for copy in copies:
        copy.wait()


def unpack_kernel(core, *refs):
    del core
    src, gq, gk = refs[0], refs[-2], refs[-1]

    def head(h):
        state, _ = get_state(src, h)
        gq[h] = state[:64]
        gk[h] = state[64:]
        yield

    return head


class Block:
    def __init__(self, shape, view, cut=None):
        self.shape = shape
        self.view = view
        self.cut = cut or (lambda ref, core, start, count: view(ref, start, count))


def heads_block(*tail):
    return Block((HALF,) + tail, lambda ref, start, count: ref.at[pl.ds(start, count)])


def core_heads(*tail, other=False):
    def cut(ref, core, start, count):
        return ref.at[pl.ds(((1 - core) if other else core) * HALF + start, count)]

    return Block((HALF,) + tail, heads_block(*tail).view, cut)


def group_columns(core_part=None):
    def view(ref, start, count):
        return ref.at[:, pl.ds(start * WIDTH, count * WIDTH)]

    def cut(ref, core, start, count):
        side = core if core_part == "own" else 1 - core
        at = pl.multiple_of(side * HALF * WIDTH + start * WIDTH, WIDTH)
        return ref.at[:, pl.ds(at, count * WIDTH)]

    return Block((ROWS, HALF * WIDTH), view, cut if core_part else None)


def pieces_block():
    def view(ref, start, count):
        return ref.at[pl.ds(start // 2, count // 2)]

    return Block((PAIRS, PROWS, WIDTH), view)


def is_block(spec):
    return isinstance(spec, Block)


def stream(*refs, body, ins, outs, n_out, groups, backward):
    core = refs[0][0]
    arrays = refs[1 : 1 + len(ins)]
    results = refs[1 + len(ins) : 1 + len(ins) + n_out]
    in_sems, out_sems, *buffers = refs[1 + len(ins) + n_out :]
    given = [buffers.pop(0) if is_block(spec) else ref for spec, ref in zip(ins, arrays)]
    streamed = [at for at, _ in outs]
    whole = [ref for n, ref in enumerate(results) if n not in streamed]
    heads = list(range(HALF))
    if backward:
        heads.reverse()

    def spans_of(counts):
        spans = []
        for g, count in enumerate(counts):
            part = heads[sum(counts[:g]) : sum(counts[:g]) + count]
            spans.append((min(part), count))
        return spans

    spans_in, spans_out = spans_of(groups[0]), spans_of(groups[1])

    def copies_in(g):
        return [
            pltpu.make_async_copy(
                spec.cut(ref, core, *spans_in[g]), spec.view(buf, *spans_in[g]), in_sems.at[n, g]
            )
            for n, (spec, ref, buf) in enumerate(zip(ins, arrays, given))
            if is_block(spec)
        ]

    def copies_out(g):
        return [
            pltpu.make_async_copy(
                spec.view(buf, *spans_out[g]),
                spec.cut(results[at], core, *spans_out[g]),
                out_sems.at[n, g],
            )
            for n, ((at, spec), buf) in enumerate(zip(outs, buffers))
        ]

    for g in range(len(spans_in)):
        for copy in copies_in(g):
            copy.start()
    head = body(core, *given, *buffers, *whole)
    done = 0
    ends = [sum(groups[1][: g + 1]) for g in range(len(spans_out))]

    running = []

    def advance():
        nonlocal done
        for item in list(running):
            if next(item, "end") == "end":
                running.remove(item)
                done += 1
                if done in ends:
                    for copy in copies_out(ends.index(done)):
                        copy.start()

    for g, (_, count) in enumerate(spans_in):
        for copy in copies_in(g):
            copy.wait()
        for _ in range(count):
            running.append(head(heads.pop(0)))
            advance()
    while running:
        advance()
    for g in range(len(spans_out)):
        for copy in copies_out(g):
            copy.wait()


def raw_call(body, name, core, values, specs, shapes, scratch, aliases=()):
    spaces = {None: pltpu.VMEM}
    constrained = [
        pltpu.with_memory_space_constraint(v, spaces.get(s, pltpu.HBM))
        for v, s in zip(values, specs)
    ]
    return pl.pallas_call(
        body,
        in_specs=[pl.BlockSpec(memory_space=pltpu.SMEM)]
        + [pl.BlockSpec(memory_space=spaces.get(s, pltpu.HBM)) for s in specs],
        out_specs=tuple(pl.BlockSpec(memory_space=shape.memory_space) for shape in shapes),
        out_shape=tuple(shapes),
        scratch_shapes=scratch,
        name=name,
        input_output_aliases=dict(aliases),
        compiler_params=pltpu.CompilerParams(vmem_limit_bytes=48 * 1024 * 1024),
    )(core, *constrained)


def call(
    body, name, core, args, shapes, outs, aliases=(), groups=GROUPS, backward=False
):
    ins = [spec for _, spec in args]
    scratch = [
        pltpu.SemaphoreType.DMA((len(ins), len(groups[0]))),
        pltpu.SemaphoreType.DMA((len(outs), len(groups[1]))),
    ]
    scratch += [pltpu.VMEM(spec.shape, value.dtype) for value, spec in args if is_block(spec)]
    scratch += [pltpu.VMEM(spec.shape, shapes[at].dtype) for at, spec in outs]
    kernel = functools.partial(
        stream, body=body, ins=ins, outs=outs, n_out=len(shapes), groups=groups,
        backward=backward,
    )
    return raw_call(kernel, name, core, [v for v, _ in args], ins, shapes, scratch, aliases)


def sds(shape, dtype=F32):
    return pltpu.HBM(shape, dtype)


PAYLOAD = sds((PAIRS, PROWS, WIDTH))


def exchange(x):
    pieces = lax.all_to_all(x.reshape(NCHIP, 1, PIECE * WIDTH), CHIPS, 0, 0, tiled=True)
    return pieces.reshape(PAIRS, PROWS, WIDTH)


def scan(core, x, reverse):
    body = functools.partial(scan_kernel, reverse=reverse)
    return call(
        body, "scan", core, [(x, None)], [PAYLOAD], [(0, pieces_block())], backward=reverse
    )[0]


def swap(x):
    return lax.ppermute(x, "c", [(0, 1), (1, 0)])


def shards(queries, keys, values, teacher, query_map, key_map):
    c = lax.axis_index("c").astype(jnp.int32)
    core = c.reshape(1)
    half = HALF * WIDTH

    def others(x):
        part = lax.dynamic_slice(x, (0, (1 - c) * half), (ROWS, half))
        return swap(part.astype(F32))

    k_other, v_other = others(keys), others(values)
    q_other, t_other = others(queries), others(teacher)

    def run(body, name, args, results, groups=GROUPS):
        shapes = [shape for shape, _ in results]
        outs = [(n, spec) for n, (_, spec) in enumerate(results) if spec is not None]
        return call(body, name, core, args, shapes, outs, groups=groups)

    own = group_columns("own")
    cols = group_columns()
    natural = (sds((HALF, TOK, WIDTH), BF16), heads_block(TOK, WIDTH))
    features = (sds((HALF, WIDTH, TOK)), heads_block(WIDTH, TOK))
    row = (sds((HALF, 8, TOK)), heads_block(8, TOK))
    grads = (sds((HALF, 64, WIDTH)), heads_block(64, WIDTH))
    weight = core_heads(64, WIDTH)
    payload = (PAYLOAD, pieces_block())
    lossy = (pltpu.VMEM((8, WIDTH), F32), None)

    kf, vf, phik, send = run(
        key_kernel, "keys",
        [(keys, own), (k_other, None), (values, own), (v_other, None), (key_map, weight)],
        [natural, natural, features, payload],
    )
    gathered = exchange(send)
    qf, phiq, phiqb, den, num = run(
        score_kernel, "scores",
        [(queries, own), (q_other, cols), (query_map, weight), (phik, features[1]),
         (vf, natural[1])],
        [natural, features, natural, row, (pltpu.VMEM((HALF, TOK, WIDTH), F32), None)],
    )
    pre = exchange(scan(core, gathered, False))
    y_own, y_send, dnum, dden, send, loss = run(
        out_kernel, "outs",
        [(pre, None), (num, None), (phiq, features[1]), (phiqb, natural[1]), (den, row[1]),
         (teacher, own), (t_other, cols)],
        [(sds((ROWS, half), BF16), cols), (sds((ROWS, half)), cols), natural, row, payload,
         lossy],
    )
    loss_other = swap(loss)
    gathered = exchange(send)
    grad_query, dphik = run(
        grid_kernel, "grids",
        [(dnum, natural[1]), (vf, natural[1]), (dden, row[1]), (phiq, features[1]),
         (phik, features[1]), (pre, payload[1]), (qf, natural[1])],
        [grads, (pltpu.VMEM((HALF, WIDTH, TOK), F32), None)],
    )
    gathered, dphik, grad_query, y_send = lax.optimization_barrier(
        (gathered, dphik, grad_query, y_send)
    )
    y_other = swap(y_send)
    suf, y_other = lax.optimization_barrier((exchange(scan(core, gathered, True)), y_other))
    send, = run(
        last_kernel, "last",
        [(suf, None), (vf, natural[1]), (phik, features[1]), (kf, natural[1]),
         (dphik, None), (grad_query, grads[1]), (loss, None), (loss_other, None)],
        [payload],
    )
    attn, = call(
        merge_kernel, "merge", core, [(y_own, cols), (y_other, None)],
        [sds((ROWS, HEADS * WIDTH), BF16)],
        [(0, own), (0, group_columns("other"))],
    )
    gathered, attn = lax.optimization_barrier((exchange(send), attn))
    spread, = raw_call(
        sum_kernel, "sum", core, [gathered], [None], [PAYLOAD],
        [pltpu.VMEM((PROWS, WIDTH), F32), pltpu.SemaphoreType.DMA((PAIRS,))],
    )
    total = exchange(spread)
    theirs = swap(total)
    loss = jnp.sum(total[0, 32]) * (1.0 / (HEADS * WIDTH) / (NCHIP * TOK))
    grad = sds((HEADS, 64, WIDTH))
    mine, other = core_heads(64, WIDTH), core_heads(64, WIDTH, other=True)
    grad_query, grad_key = call(
        unpack_kernel, "unpack_mine", core, [(total, None)], [grad, grad],
        [(0, mine), (1, mine)],
    )
    grad_query, grad_key = call(
        unpack_kernel, "unpack", core,
        [(theirs, None), (grad_query, pltpu.HBM), (grad_key, pltpu.HBM)], [grad, grad],
        [(0, other), (1, other)], aliases=[(2, 0), (3, 1)],
    )
    return attn, loss, grad_query, grad_key


def solution(mesh):
    fine = Mesh(mesh.devices.reshape(4, 4, 4, 2), ("x", "z", "y", "c"))
    tokens = P(("x", "z", "y", "c"), None)
    return jax.shard_map(
        shards,
        mesh=fine,
        in_specs=(tokens, tokens, tokens, tokens, P(), P()),
        out_specs=(tokens, P(), P(), P()),
        check_vma=False,
    )
```

```python
import functools

import jax
import jax.numpy as jnp
from jax import lax
from jax.experimental import pallas as pl
from jax.experimental.pallas import tpu as pltpu
from jax.sharding import Mesh
from jax.sharding import PartitionSpec as P

F32 = jnp.float32
BF16 = jnp.bfloat16
CHIPS = ("x", "z", "y")
NCHIP = 64
HEADS = 32
HALF = 16
ROWS = 128
TOK = 256
WIDTH = 128
PIECE = 33
PAIRS = HALF // 2
GROUPS = ((8, 8), (12, 4))
PROWS = 2 * 4 * PIECE

NN = ((1,), (0,))
NT = ((1,), (1,))


def dot(a, b, dims=NN):
    return lax.dot_general(a, b, (dims, ((), ())), preferred_element_type=F32)


def two_parts(x):
    high = x.astype(BF16)
    return high, (x - high.astype(F32)).astype(BF16)


def soft_maps(logits):
    e_one = jnp.exp(logits - jnp.max(logits, axis=0, keepdims=True))
    e_two = jnp.exp(jnp.min(logits, axis=0, keepdims=True) - logits)
    one = e_one * (1.0 / jnp.sum(e_one, axis=0, keepdims=True))
    two = e_two * (1.0 / jnp.sum(e_two, axis=0, keepdims=True))
    return jnp.concatenate([one, two], axis=0)


def soft_back(phi, dphi, x, rounded=False):
    halves = []
    for part in (slice(0, 64), slice(64, 128)):
        prod = phi[part] * dphi[part]
        mean = jnp.sum(prod, axis=0, keepdims=True)
        if rounded:
            mean = mean * (1.0 / jnp.sum(phi[part], axis=0, keepdims=True))
        halves.append(prod - phi[part] * mean)
    return dot((halves[0] - halves[1]).astype(BF16), x)


def columns(h):
    return slice(h * WIDTH, (h + 1) * WIDTH)


def both_cores(own, other, h):
    return jnp.concatenate(
        [own[:, columns(h)], other[:, columns(h)].astype(BF16)], axis=0
    )


def put_state(ref, h, state, row):
    pair = h // 2
    for q in range(4):
        at = (4 * (h % 2) + q) * PIECE
        ref[pair, at : at + 32, :] = state[32 * q : 32 * q + 32]
        ref[pair, at + 32 : at + 33, :] = row


def put_grad(ref, h, grad, row):
    for q in range(2):
        at = (2 * (h % 4) + q) * PIECE
        ref[h // 4, at : at + 32, :] = grad[32 * q : 32 * q + 32]
        ref[h // 4, at + 32 : at + 33, :] = row


def get_grad(ref, h, side):
    at = 2 * (h % 4) * PIECE
    parts = [ref[h // 4, side, at + q * PIECE : at + q * PIECE + 32, :] for q in range(2)]
    return jnp.concatenate(parts, axis=0)


def get_state(ref, h):
    first = 4 * (h % 2)
    parts = [ref[h // 2, (first + q) * PIECE : (first + q) * PIECE + 32, :] for q in range(4)]
    at = first * PIECE + 32
    return jnp.concatenate(parts, axis=0), ref[h // 2, at : at + 1, :]


def as_column(row, lanes):
    return jnp.broadcast_to(row, (lanes, row.shape[1])).T


def twice(x):
    return jnp.concatenate([x, x], axis=1)


def causal(core):
    shift = core * ROWS
    at_query = lax.broadcasted_iota(jnp.int32, (TOK, TOK), 0) ^ shift
    at_key = lax.broadcasted_iota(jnp.int32, (TOK, TOK), 1) ^ shift
    return at_query >= at_key


def key_kernel(core, k_own, k_other, v_own, v_other, w_ref, phik_ref, send):
    ones = jnp.ones((8, 2 * TOK), BF16)

    def head(h):
        logits = dot(w_ref[h], both_cores(k_own, k_other, h), NT)
        yield
        phik = soft_maps(logits)
        phikb, low = two_parts(phik)
        phik_ref[h] = phikb
        yield
        state = dot(phikb, both_cores(v_own, v_other, h))
        row = dot(ones, jnp.concatenate([phikb, low], axis=1), NT)[:1]
        yield
        put_state(send, h, state, row)

    return head


def pack_kernel(core, k_own, k_other, v_own, v_other, kf, vf):
    def head(h):
        kf[h] = both_cores(k_own, k_other, h)
        vf[h] = both_cores(v_own, v_other, h)
        yield

    return head


def score_kernel(
    core, q_own, q_other, w_ref, phik_ref, vf, t_own, t_other,
    qf, phiq_ref, phiqb_ref, tf, den_ref, num_ref,
):
    mask = causal(core)
    ones = jnp.ones((8, 2 * TOK), BF16)

    def head(h):
        q = both_cores(q_own, q_other, h)
        qf[h] = q
        logits = dot(w_ref[h], q, NT)
        yield
        phiq = soft_maps(logits)
        phiq_ref[h] = phiq
        phiqb = phiq.astype(BF16).T
        phiqb_ref[h] = phiqb
        tf[h] = both_cores(t_own, t_other, h)
        yield
        scores = dot(phiqb, phik_ref[h])
        yield
        high, low = two_parts(jnp.where(mask, scores, 0.0))
        num_ref[h] = dot(high, vf[h])
        den_ref[h] = dot(ones, jnp.concatenate([high, low], axis=1), NT)

    return head


def out_kernel(
    core, pre, num_ref, phiq_ref, phiqb_ref, den_ref, tf,
    y_own, y_send, dnum_ref, dden_ref, send, loss_ref,
):
    ones = jnp.ones((8, 2 * WIDTH), BF16)
    wide = jnp.ones((8, 2 * TOK), BF16)
    scale = 2.0 / (HEADS * WIDTH)
    loss_ref[...] = jnp.zeros_like(loss_ref)

    def head(h):
        state, norm = get_state(pre, h)
        carried = dot(phiqb_ref[h], state.astype(BF16))
        down = as_column(norm, WIDTH)
        yield
        phiq = phiq_ref[h]
        before = jnp.sum(phiq * twice(down), axis=0, keepdims=True)
        inv = as_column(1.0 / (den_ref[h][:1] + before), WIDTH)
        yield
        y = (num_ref[h] + carried) * inv
        y_own[:, columns(h)] = y[:ROWS].astype(BF16)
        y_send[:, columns(h)] = y[ROWS:]
        err = y - tf[h].astype(F32)
        loss_ref[...] += jnp.sum((err * err).reshape(TOK // 8, 8, WIDTH), axis=0)
        dnum = (scale * err) * inv
        dnumb = dnum.astype(BF16)
        dnum_ref[h] = dnumb
        high, low = two_parts(dnum * y)
        both = jnp.concatenate([high, low], axis=1)
        yield
        dden = -dot(ones, both, NT)
        rev = dot(phiq_ref[h].astype(BF16), dnumb)
        yield
        dden_ref[h] = dden
        high, low = two_parts(phiq_ref[h] * dden[:1])
        yield
        rnorm = dot(wide, jnp.concatenate([high, low], axis=1), NT)
        yield
        put_state(send, h, rev, rnorm[:1])

    return head


def grid_kernel(
    core, dnum_ref, vf, dden_ref, phiq_ref, phik_ref, pre, qf, send, dphik_ref,
):
    mask = causal(core)

    def head(h):
        grid = dot(dnum_ref[h], vf[h], NT)
        column = as_column(dden_ref[h][:1], WIDTH)
        yield
        gridb = jnp.where(mask, grid + twice(column), 0.0).astype(BF16)
        dphik_ref[h] = dot(phiq_ref[h].astype(BF16), gridb)
        state, norm = get_state(pre, h)
        left = jnp.concatenate([phik_ref[h], state.astype(BF16)], axis=1)
        dphiq = dot(left, jnp.concatenate([gridb, dnum_ref[h]], axis=1), NT)
        down = twice(as_column(norm, WIDTH))
        yield
        grad = soft_back(phiq_ref[h], dphiq + down * dden_ref[h][:1], qf[h])
        put_grad(send, h, grad, jnp.zeros((1, WIDTH), F32))

    return head


def merge_kernel(core, y_own, y_other, attn_mine, attn_theirs):
    del core

    def head(h):
        attn_mine[:, columns(h)] = y_own[:, columns(h)]
        attn_theirs[:, columns(h)] = y_other[:, columns(h)].astype(BF16)
        yield

    return head


def last_kernel(
    core, suf, vf, phik_ref, kf, dphik_ref, loss_ref, loss_other, queries_sent, send
):
    del queries_sent
    row = jnp.sum(loss_ref[...] + loss_other[...], axis=0, keepdims=True)

    def head(h):
        state, norm = get_state(suf, h)
        carried = dot(state.astype(BF16), vf[h], NT) + twice(as_column(norm, WIDTH))
        yield
        grad_key = soft_back(
            phik_ref[h].astype(F32), dphik_ref[h] + carried, kf[h], rounded=True
        )
        yield
        put_grad(send, h, grad_key, row)

    return head


def scan_kernel(core, x_ref, o_ref, *, reverse):
    del core
    acc = jnp.zeros((PIECE, WIDTH), F32)

    def head(h):
        nonlocal acc
        for j in range(3, -1, -1) if reverse else range(4):
            at = (4 * (h % 2) + j) * PIECE
            o_ref[h // 2, at : at + PIECE, :] = acc
            acc = acc + x_ref[h // 2, at : at + PIECE, :]
        yield

    return head


def sum_kernel(core_ref, x_ref, o_ref, buf, sems):
    del core_ref
    parts = []
    for b in range(PAIRS):
        part = x_ref[b, :PIECE, :]
        for j in range(1, 8):
            part = part + x_ref[b, PIECE * j : PIECE * (j + 1), :]
        parts.append(part)
    while len(parts) > 1:
        parts = [x + y for x, y in zip(parts[::2], parts[1::2])]
    for j in range(8):
        buf[PIECE * j : PIECE * (j + 1), :] = parts[0]
    copies = [pltpu.make_async_copy(buf, o_ref.at[b], sems.at[b]) for b in range(PAIRS)]
    for copy in copies:
        copy.start()
    for copy in copies:
        copy.wait()


def unpack_kernel(core, *refs):
    del core
    src, gq, gk = refs[0], refs[-2], refs[-1]

    def head(h):
        gq[h] = get_grad(src, h, 0)
        gk[h] = get_grad(src, h, 1)
        yield

    return head


class Block:
    def __init__(self, shape, view, cut=None):
        self.shape = shape
        self.view = view
        self.cut = cut or (lambda ref, core, start, count: view(ref, start, count))


def heads_block(*tail):
    return Block((HALF,) + tail, lambda ref, start, count: ref.at[pl.ds(start, count)])


def core_heads(*tail, other=False):
    def cut(ref, core, start, count):
        return ref.at[pl.ds(((1 - core) if other else core) * HALF + start, count)]

    return Block((HALF,) + tail, heads_block(*tail).view, cut)


def group_columns(core_part=None):
    def view(ref, start, count):
        return ref.at[:, pl.ds(start * WIDTH, count * WIDTH)]

    def cut(ref, core, start, count):
        side = core if core_part == "own" else 1 - core
        at = pl.multiple_of(side * HALF * WIDTH + start * WIDTH, WIDTH)
        return ref.at[:, pl.ds(at, count * WIDTH)]

    return Block((ROWS, HALF * WIDTH), view, cut if core_part else None)


def pieces_block():
    def view(ref, start, count):
        return ref.at[pl.ds(start // 2, count // 2)]

    return Block((PAIRS, PROWS, WIDTH), view)


def is_block(spec):
    return isinstance(spec, Block)


def stream(*refs, body, ins, outs, n_out, groups, backward):
    core = refs[0][0]
    arrays = refs[1 : 1 + len(ins)]
    results = refs[1 + len(ins) : 1 + len(ins) + n_out]
    in_sems, out_sems, *buffers = refs[1 + len(ins) + n_out :]
    given = [buffers.pop(0) if is_block(spec) else ref for spec, ref in zip(ins, arrays)]
    streamed = [at for at, _ in outs]
    whole = [ref for n, ref in enumerate(results) if n not in streamed]
    heads = list(range(HALF))
    if backward:
        heads.reverse()

    def spans_of(counts):
        spans = []
        for g, count in enumerate(counts):
            part = heads[sum(counts[:g]) : sum(counts[:g]) + count]
            spans.append((min(part), count))
        return spans

    spans_in, spans_out = spans_of(groups[0]), spans_of(groups[1])

    def copies_in(g):
        return [
            pltpu.make_async_copy(
                spec.cut(ref, core, *spans_in[g]), spec.view(buf, *spans_in[g]), in_sems.at[n, g]
            )
            for n, (spec, ref, buf) in enumerate(zip(ins, arrays, given))
            if is_block(spec)
        ]

    def copies_out(g):
        return [
            pltpu.make_async_copy(
                spec.view(buf, *spans_out[g]),
                spec.cut(results[at], core, *spans_out[g]),
                out_sems.at[n, g],
            )
            for n, ((at, spec), buf) in enumerate(zip(outs, buffers))
        ]

    for g in range(len(spans_in)):
        for copy in copies_in(g):
            copy.start()
    head = body(core, *given, *buffers, *whole)
    done = 0
    ends = [sum(groups[1][: g + 1]) for g in range(len(spans_out))]

    running = []

    def advance():
        nonlocal done
        for item in list(running):
            if next(item, "end") == "end":
                running.remove(item)
                done += 1
                if done in ends:
                    for copy in copies_out(ends.index(done)):
                        copy.start()

    for g, (_, count) in enumerate(spans_in):
        for copy in copies_in(g):
            copy.wait()
        for _ in range(count):
            running.append(head(heads.pop(0)))
            advance()
    while running:
        advance()
    for g in range(len(spans_out)):
        for copy in copies_out(g):
            copy.wait()


def quads_block(side):
    def view(ref, start, count):
        return ref.at[pl.ds(start // 4, count // 4)]

    def cut(ref, core, start, count):
        return ref.at[pl.ds(start // 4, count // 4), side]

    return Block((HALF // 4, PROWS, WIDTH), view, cut)


def raw_call(body, name, core, values, specs, shapes, scratch, aliases=()):
    spaces = {None: pltpu.VMEM}
    constrained = [
        pltpu.with_memory_space_constraint(v, spaces.get(s, pltpu.HBM))
        for v, s in zip(values, specs)
    ]
    return pl.pallas_call(
        body,
        in_specs=[pl.BlockSpec(memory_space=pltpu.SMEM)]
        + [pl.BlockSpec(memory_space=spaces.get(s, pltpu.HBM)) for s in specs],
        out_specs=tuple(pl.BlockSpec(memory_space=shape.memory_space) for shape in shapes),
        out_shape=tuple(shapes),
        scratch_shapes=scratch,
        name=name,
        input_output_aliases=dict(aliases),
        compiler_params=pltpu.CompilerParams(vmem_limit_bytes=48 * 1024 * 1024),
    )(core, *constrained)


def call(
    body, name, core, args, shapes, outs, aliases=(), groups=GROUPS, backward=False
):
    ins = [spec for _, spec in args]
    scratch = [
        pltpu.SemaphoreType.DMA((len(ins), len(groups[0]))),
        pltpu.SemaphoreType.DMA((len(outs), len(groups[1]))),
    ]
    scratch += [pltpu.VMEM(spec.shape, value.dtype) for value, spec in args if is_block(spec)]
    scratch += [pltpu.VMEM(spec.shape, shapes[at].dtype) for at, spec in outs]
    kernel = functools.partial(
        stream, body=body, ins=ins, outs=outs, n_out=len(shapes), groups=groups,
        backward=backward,
    )
    return raw_call(kernel, name, core, [v for v, _ in args], ins, shapes, scratch, aliases)


def sds(shape, dtype=F32):
    return pltpu.HBM(shape, dtype)


PAYLOAD = sds((PAIRS, PROWS, WIDTH))


GRADS = sds((HALF // 4, 2, PROWS, WIDTH))


def exchange(x):
    pieces = lax.all_to_all(x.reshape(NCHIP, 1, PIECE * WIDTH), CHIPS, 0, 0, tiled=True)
    return pieces.reshape(PAIRS, PROWS, WIDTH)


def scan(core, x, reverse):
    body = functools.partial(scan_kernel, reverse=reverse)
    return call(
        body, "scan", core, [(x, None)], [PAYLOAD], [(0, pieces_block())], backward=reverse
    )[0]


def swap(x):
    return lax.ppermute(x, "c", [(0, 1), (1, 0)])


def shards(queries, keys, values, teacher, query_map, key_map):
    c = lax.axis_index("c").astype(jnp.int32)
    core = c.reshape(1)
    half = HALF * WIDTH

    def others(x):
        part = lax.dynamic_slice(x, (0, (1 - c) * half), (ROWS, half))
        return swap(part.astype(F32))

    k_other, v_other = others(keys), others(values)
    q_other, t_other = others(queries), others(teacher)

    def run(body, name, args, results, groups=GROUPS):
        shapes = [shape for shape, _ in results]
        outs = [(n, spec) for n, (_, spec) in enumerate(results) if spec is not None]
        return call(body, name, core, args, shapes, outs, groups=groups)

    own = group_columns("own")
    cols = group_columns()
    natural = (sds((HALF, TOK, WIDTH), BF16), heads_block(TOK, WIDTH))
    features = (sds((HALF, WIDTH, TOK)), heads_block(WIDTH, TOK))
    row = (sds((HALF, 8, TOK)), heads_block(8, TOK))
    weight = core_heads(64, WIDTH)
    payload = (PAYLOAD, pieces_block())
    lossy = (pltpu.VMEM((8, WIDTH), F32), None)

    halved = (sds((HALF, WIDTH, TOK), BF16), heads_block(WIDTH, TOK))
    swapped = [(keys, own), (k_other, None), (values, own), (v_other, None)]
    phik, send = run(key_kernel, "keys", swapped + [(key_map, weight)], [halved, payload])
    gathered = exchange(send)
    kf, vf = run(pack_kernel, "pack", swapped, [natural, natural])
    gathered, kf, vf, q_other, t_other = lax.optimization_barrier(
        (gathered, kf, vf, q_other, t_other)
    )
    qf, phiq, phiqb, tf, den, num = run(
        score_kernel, "scores",
        [(queries, own), (q_other, cols), (query_map, weight), (phik, halved[1]),
         (vf, natural[1]), (teacher, own), (t_other, cols)],
        [natural, features, natural, natural, row, (pltpu.VMEM((HALF, TOK, WIDTH), F32), None)],
    )
    pre = exchange(scan(core, gathered, False))
    y_own, y_send, dnum, dden, send, loss = run(
        out_kernel, "outs",
        [(pre, None), (num, None), (phiq, features[1]), (phiqb, natural[1]), (den, row[1]),
         (tf, natural[1])],
        [(sds((ROWS, half), BF16), cols), (sds((ROWS, half)), cols), natural, row, payload,
         lossy],
        groups=((6, 10), (12, 4)),
    )
    loss_other = swap(loss)
    gathered = exchange(send)
    query_sent, dphik = run(
        grid_kernel, "grids",
        [(dnum, natural[1]), (vf, natural[1]), (dden, row[1]), (phiq, features[1]),
         (phik, halved[1]), (pre, payload[1]), (qf, natural[1])],
        [(GRADS, quads_block(0)), (pltpu.VMEM((HALF, WIDTH, TOK), F32), None)],
    )
    gathered, dphik, query_sent, y_send = lax.optimization_barrier(
        (gathered, dphik, query_sent, y_send)
    )
    y_other = swap(y_send)
    suf, y_other = lax.optimization_barrier((exchange(scan(core, gathered, True)), y_other))
    send, = call(
        last_kernel, "last", core,
        [(suf, None), (vf, natural[1]), (phik, halved[1]), (kf, natural[1]), (dphik, None),
         (loss, None), (loss_other, None), (query_sent, pltpu.HBM)],
        [GRADS], [(0, quads_block(1))], aliases=[(8, 0)],
    )
    attn, = call(
        merge_kernel, "merge", core, [(y_own, cols), (y_other, None)],
        [sds((ROWS, HEADS * WIDTH), BF16)],
        [(0, own), (0, group_columns("other"))],
    )
    gathered, attn = lax.optimization_barrier((exchange(send), attn))
    spread, = raw_call(
        sum_kernel, "sum", core, [gathered], [None], [PAYLOAD],
        [pltpu.VMEM((PROWS, WIDTH), F32), pltpu.SemaphoreType.DMA((PAIRS,))],
    )
    total = exchange(spread).reshape(GRADS.shape)
    theirs = swap(total)
    loss = jnp.sum(total[0, 1, 32]) * (1.0 / (HEADS * WIDTH) / (NCHIP * TOK))
    grad = sds((HEADS, 64, WIDTH))
    mine, other = core_heads(64, WIDTH), core_heads(64, WIDTH, other=True)
    grad_query, grad_key = call(
        unpack_kernel, "unpack_mine", core, [(total, None)], [grad, grad],
        [(0, mine), (1, mine)],
    )
    grad_query, grad_key = call(
        unpack_kernel, "unpack", core,
        [(theirs, None), (grad_query, pltpu.HBM), (grad_key, pltpu.HBM)], [grad, grad],
        [(0, other), (1, other)], aliases=[(2, 0), (3, 1)],
    )
    return attn, loss, grad_query, grad_key


def solution(mesh):
    fine = Mesh(mesh.devices.reshape(4, 4, 4, 2), ("x", "z", "y", "c"))
    tokens = P(("x", "z", "y", "c"), None)
    return jax.shard_map(
        shards,
        mesh=fine,
        in_specs=(tokens, tokens, tokens, tokens, P(), P()),
        out_specs=(tokens, P(), P(), P()),
        check_vma=False,
    )
```

```python
import functools

import jax
import jax.numpy as jnp
from jax import lax
from jax.experimental import pallas as pl
from jax.experimental.pallas import tpu as pltpu
from jax.sharding import Mesh
from jax.sharding import PartitionSpec as P

F32 = jnp.float32
BF16 = jnp.bfloat16
CHIPS = ("x", "z", "y")
NCHIP = 64
HEADS = 32
HALF = 16
ROWS = 128
TOK = 256
WIDTH = 128
PIECE = 33
PAIRS = HALF // 2
GROUPS = ((8, 8), (4, 4, 4, 4))
PROWS = 2 * 4 * PIECE

NN = ((1,), (0,))
NT = ((1,), (1,))


def dot(a, b, dims=NN):
    return lax.dot_general(a, b, (dims, ((), ())), preferred_element_type=F32)


def two_parts(x):
    high = x.astype(BF16)
    return high, (x - high.astype(F32)).astype(BF16)


def soft_maps(logits):
    e_one = jnp.exp(logits - jnp.max(logits, axis=0, keepdims=True))
    e_two = jnp.exp(jnp.min(logits, axis=0, keepdims=True) - logits)
    one = e_one * (1.0 / jnp.sum(e_one, axis=0, keepdims=True))
    two = e_two * (1.0 / jnp.sum(e_two, axis=0, keepdims=True))
    return jnp.concatenate([one, two], axis=0)


def soft_back(phi, dphi, x, rounded=False):
    halves = []
    for part in (slice(0, 64), slice(64, 128)):
        prod = phi[part] * dphi[part]
        mean = jnp.sum(prod, axis=0, keepdims=True)
        if rounded:
            mean = mean * (1.0 / jnp.sum(phi[part], axis=0, keepdims=True))
        halves.append(prod - phi[part] * mean)
    return dot((halves[0] - halves[1]).astype(BF16), x)


def columns(h):
    return slice(h * WIDTH, (h + 1) * WIDTH)


def both_cores(own, other, h):
    return jnp.concatenate(
        [own[:, columns(h)], other[:, columns(h)].astype(BF16)], axis=0
    )


def put_state(ref, h, state, row):
    pair = h // 2
    for q in range(4):
        at = (4 * (h % 2) + q) * PIECE
        ref[pair, at : at + 32, :] = state[32 * q : 32 * q + 32]
        ref[pair, at + 32 : at + 33, :] = row


def put_grad(ref, h, grad, row):
    for q in range(2):
        at = (2 * (h % 4) + q) * PIECE
        ref[h // 4, at : at + 32, :] = grad[32 * q : 32 * q + 32]
        ref[h // 4, at + 32 : at + 33, :] = row


def get_grad(ref, h, side):
    at = 2 * (h % 4) * PIECE
    parts = [ref[h // 4, side, at + q * PIECE : at + q * PIECE + 32, :] for q in range(2)]
    return jnp.concatenate(parts, axis=0)


def get_state(ref, h):
    first = 4 * (h % 2)
    parts = [ref[h // 2, (first + q) * PIECE : (first + q) * PIECE + 32, :] for q in range(4)]
    at = first * PIECE + 32
    return jnp.concatenate(parts, axis=0), ref[h // 2, at : at + 1, :]


def as_column(row, lanes):
    return jnp.broadcast_to(row, (lanes, row.shape[1])).T


def twice(x):
    return jnp.concatenate([x, x], axis=1)


def causal(core):
    shift = core * ROWS
    at_query = lax.broadcasted_iota(jnp.int32, (TOK, TOK), 0) ^ shift
    at_key = lax.broadcasted_iota(jnp.int32, (TOK, TOK), 1) ^ shift
    return at_query >= at_key


def key_kernel(core, k_own, k_other, v_own, v_other, w_ref, phik_ref, send):
    ones = jnp.ones((8, 2 * TOK), BF16)

    def head(h):
        logits = dot(w_ref[h], both_cores(k_own, k_other, h), NT)
        yield
        phik = soft_maps(logits)
        phikb, low = two_parts(phik)
        phik_ref[h] = phikb
        yield
        state = dot(phikb, both_cores(v_own, v_other, h))
        row = dot(ones, jnp.concatenate([phikb, low], axis=1), NT)[:1]
        yield
        put_state(send, h, state, row)

    return head


def pack_kernel(core, k_own, k_other, v_own, v_other, kf, vf):
    def head(h):
        kf[h] = both_cores(k_own, k_other, h)
        vf[h] = both_cores(v_own, v_other, h)
        yield

    return head


def score_kernel(
    core, q_own, q_other, w_ref, phik_ref, vf, t_own, t_other,
    qf, phiq_ref, phiqb_ref, tf, den_ref, num_ref,
):
    mask = causal(core)
    ones = jnp.ones((8, 2 * TOK), BF16)

    def head(h):
        q = both_cores(q_own, q_other, h)
        qf[h] = q
        logits = dot(w_ref[h], q, NT)
        yield
        phiq = soft_maps(logits)
        phiq_ref[h] = phiq
        phiqb = phiq.astype(BF16).T
        phiqb_ref[h] = phiqb
        tf[h] = both_cores(t_own, t_other, h)
        yield
        scores = dot(phiqb, phik_ref[h])
        yield
        high, low = two_parts(jnp.where(mask, scores, 0.0))
        num_ref[h] = dot(high, vf[h])
        den_ref[h] = dot(ones, jnp.concatenate([high, low], axis=1), NT)

    return head


def out_kernel(
    core, pre, num_ref, phiq_ref, phiqb_ref, den_ref, tf,
    y_own, y_send, dnum_ref, dden_ref, send, loss_ref,
):
    ones = jnp.ones((8, 2 * WIDTH), BF16)
    wide = jnp.ones((8, 2 * TOK), BF16)
    scale = 2.0 / (HEADS * WIDTH)
    loss_ref[...] = jnp.zeros_like(loss_ref)

    def head(h):
        state, norm = get_state(pre, h)
        carried = dot(phiqb_ref[h], state.astype(BF16))
        down = as_column(norm, WIDTH)
        yield
        phiq = phiq_ref[h]
        before = jnp.sum(phiq * twice(down), axis=0, keepdims=True)
        inv = as_column(1.0 / (den_ref[h][:1] + before), WIDTH)
        yield
        y = (num_ref[h] + carried) * inv
        y_own[:, columns(h)] = y[:ROWS].astype(BF16)
        y_send[:, columns(h)] = y[ROWS:].astype(BF16)
        err = y - tf[h].astype(F32)
        loss_ref[...] += jnp.sum((err * err).reshape(TOK // 8, 8, WIDTH), axis=0)
        dnum = (scale * err) * inv
        dnumb = dnum.astype(BF16)
        dnum_ref[h] = dnumb
        high, low = two_parts(dnum * y)
        both = jnp.concatenate([high, low], axis=1)
        yield
        dden = -dot(ones, both, NT)
        rev = dot(phiq_ref[h].astype(BF16), dnumb)
        yield
        dden_ref[h] = dden
        high, low = two_parts(phiq_ref[h] * dden[:1])
        yield
        rnorm = dot(wide, jnp.concatenate([high, low], axis=1), NT)
        yield
        put_state(send, h, rev, rnorm[:1])

    return head


def grid_kernel(
    core, dnum_ref, vf, dden_ref, phiq_ref, phik_ref, pre, qf, send, dphik_ref,
):
    mask = causal(core)

    def head(h):
        grid = dot(dnum_ref[h], vf[h], NT)
        column = as_column(dden_ref[h][:1], WIDTH)
        yield
        gridb = jnp.where(mask, grid + twice(column), 0.0).astype(BF16)
        dphik_ref[h] = dot(phiq_ref[h].astype(BF16), gridb)
        state, norm = get_state(pre, h)
        left = jnp.concatenate([phik_ref[h], state.astype(BF16)], axis=1)
        dphiq = dot(left, jnp.concatenate([gridb, dnum_ref[h]], axis=1), NT)
        down = twice(as_column(norm, WIDTH))
        yield
        grad = soft_back(phiq_ref[h], dphiq + down * dden_ref[h][:1], qf[h])
        put_grad(send, h, grad, jnp.zeros((1, WIDTH), F32))

    return head


def merge_kernel(core, y_own, y_other, attn_mine, attn_theirs):
    del core

    def head(h):
        attn_mine[:, columns(h)] = y_own[:, columns(h)]
        attn_theirs[:, columns(h)] = y_other[:, columns(h)].astype(BF16)
        yield

    return head


def last_kernel(
    core, suf, vf, phik_ref, kf, dphik_ref, loss_ref, loss_other, queries_sent, send
):
    del queries_sent
    row = jnp.sum(loss_ref[...] + loss_other[...], axis=0, keepdims=True)

    def head(h):
        state, norm = get_state(suf, h)
        carried = dot(state.astype(BF16), vf[h], NT) + twice(as_column(norm, WIDTH))
        yield
        grad_key = soft_back(
            phik_ref[h].astype(F32), dphik_ref[h] + carried, kf[h], rounded=True
        )
        yield
        put_grad(send, h, grad_key, row)

    return head


def scan_kernel(core, x_ref, o_ref, *, reverse):
    del core
    acc = jnp.zeros((PIECE, WIDTH), F32)

    def head(h):
        nonlocal acc
        for j in range(3, -1, -1) if reverse else range(4):
            at = (4 * (h % 2) + j) * PIECE
            o_ref[h // 2, at : at + PIECE, :] = acc
            acc = acc + x_ref[h // 2, at : at + PIECE, :]
        yield

    return head


def sum_kernel(core_ref, x_ref, o_ref, buf, sems):
    del core_ref
    parts = []
    for b in range(PAIRS):
        part = x_ref[b, :PIECE, :]
        for j in range(1, 8):
            part = part + x_ref[b, PIECE * j : PIECE * (j + 1), :]
        parts.append(part)
    while len(parts) > 1:
        parts = [x + y for x, y in zip(parts[::2], parts[1::2])]
    for j in range(8):
        buf[PIECE * j : PIECE * (j + 1), :] = parts[0]
    copies = [pltpu.make_async_copy(buf, o_ref.at[b], sems.at[b]) for b in range(PAIRS)]
    for copy in copies:
        copy.start()
    for copy in copies:
        copy.wait()


def unpack_kernel(core, *refs):
    del core
    src, gq, gk = refs[0], refs[-2], refs[-1]

    def head(h):
        gq[h] = get_grad(src, h, 0)
        gk[h] = get_grad(src, h, 1)
        yield

    return head


class Block:
    def __init__(self, shape, view, cut=None):
        self.shape = shape
        self.view = view
        self.cut = cut or (lambda ref, core, start, count: view(ref, start, count))


def heads_block(*tail):
    return Block((HALF,) + tail, lambda ref, start, count: ref.at[pl.ds(start, count)])


def core_heads(*tail, other=False):
    def cut(ref, core, start, count):
        return ref.at[pl.ds(((1 - core) if other else core) * HALF + start, count)]

    return Block((HALF,) + tail, heads_block(*tail).view, cut)


def group_columns(core_part=None):
    def view(ref, start, count):
        return ref.at[:, pl.ds(start * WIDTH, count * WIDTH)]

    def cut(ref, core, start, count):
        side = core if core_part == "own" else 1 - core
        at = pl.multiple_of(side * HALF * WIDTH + start * WIDTH, WIDTH)
        return ref.at[:, pl.ds(at, count * WIDTH)]

    return Block((ROWS, HALF * WIDTH), view, cut if core_part else None)


def pieces_block():
    def view(ref, start, count):
        return ref.at[pl.ds(start // 2, count // 2)]

    return Block((PAIRS, PROWS, WIDTH), view)


def is_block(spec):
    return isinstance(spec, Block)


def stream(*refs, body, ins, outs, n_out, groups, backward):
    core = refs[0][0]
    arrays = refs[1 : 1 + len(ins)]
    results = refs[1 + len(ins) : 1 + len(ins) + n_out]
    in_sems, out_sems, *buffers = refs[1 + len(ins) + n_out :]
    given = [buffers.pop(0) if is_block(spec) else ref for spec, ref in zip(ins, arrays)]
    streamed = [at for at, _ in outs]
    whole = [ref for n, ref in enumerate(results) if n not in streamed]
    heads = list(range(HALF))
    if backward:
        heads.reverse()

    def spans_of(counts):
        spans = []
        for g, count in enumerate(counts):
            part = heads[sum(counts[:g]) : sum(counts[:g]) + count]
            spans.append((min(part), count))
        return spans

    spans_in, spans_out = spans_of(groups[0]), spans_of(groups[1])

    def copies_in(g):
        return [
            pltpu.make_async_copy(
                spec.cut(ref, core, *spans_in[g]), spec.view(buf, *spans_in[g]), in_sems.at[n, g]
            )
            for n, (spec, ref, buf) in enumerate(zip(ins, arrays, given))
            if is_block(spec)
        ]

    def copies_out(g):
        return [
            pltpu.make_async_copy(
                spec.view(buf, *spans_out[g]),
                spec.cut(results[at], core, *spans_out[g]),
                out_sems.at[n, g],
            )
            for n, ((at, spec), buf) in enumerate(zip(outs, buffers))
        ]

    for g in range(len(spans_in)):
        for copy in copies_in(g):
            copy.start()
    head = body(core, *given, *buffers, *whole)
    done = 0
    ends = [sum(groups[1][: g + 1]) for g in range(len(spans_out))]

    running = []

    def advance():
        nonlocal done
        for item in list(running):
            if next(item, "end") == "end":
                running.remove(item)
                done += 1
                if done in ends:
                    for copy in copies_out(ends.index(done)):
                        copy.start()

    for g, (_, count) in enumerate(spans_in):
        for copy in copies_in(g):
            copy.wait()
        for _ in range(count):
            running.append(head(heads.pop(0)))
            advance()
    while running:
        advance()
    for g in range(len(spans_out)):
        for copy in copies_out(g):
            copy.wait()


def quads_block(side):
    def view(ref, start, count):
        return ref.at[pl.ds(start // 4, count // 4)]

    def cut(ref, core, start, count):
        return ref.at[pl.ds(start // 4, count // 4), side]

    return Block((HALF // 4, PROWS, WIDTH), view, cut)


def raw_call(body, name, core, values, specs, shapes, scratch, aliases=()):
    spaces = {None: pltpu.VMEM}
    constrained = [
        pltpu.with_memory_space_constraint(v, spaces.get(s, pltpu.HBM))
        for v, s in zip(values, specs)
    ]
    return pl.pallas_call(
        body,
        in_specs=[pl.BlockSpec(memory_space=pltpu.SMEM)]
        + [pl.BlockSpec(memory_space=spaces.get(s, pltpu.HBM)) for s in specs],
        out_specs=tuple(pl.BlockSpec(memory_space=shape.memory_space) for shape in shapes),
        out_shape=tuple(shapes),
        scratch_shapes=scratch,
        name=name,
        input_output_aliases=dict(aliases),
        compiler_params=pltpu.CompilerParams(vmem_limit_bytes=48 * 1024 * 1024),
    )(core, *constrained)


def call(
    body, name, core, args, shapes, outs, aliases=(), groups=GROUPS, backward=False
):
    ins = [spec for _, spec in args]
    scratch = [
        pltpu.SemaphoreType.DMA((len(ins), len(groups[0]))),
        pltpu.SemaphoreType.DMA((len(outs), len(groups[1]))),
    ]
    scratch += [pltpu.VMEM(spec.shape, value.dtype) for value, spec in args if is_block(spec)]
    scratch += [pltpu.VMEM(spec.shape, shapes[at].dtype) for at, spec in outs]
    kernel = functools.partial(
        stream, body=body, ins=ins, outs=outs, n_out=len(shapes), groups=groups,
        backward=backward,
    )
    return raw_call(kernel, name, core, [v for v, _ in args], ins, shapes, scratch, aliases)


def sds(shape, dtype=F32):
    return pltpu.HBM(shape, dtype)


PAYLOAD = sds((PAIRS, PROWS, WIDTH))


GRADS = sds((HALF // 4, 2, PROWS, WIDTH))


def exchange(x):
    pieces = lax.all_to_all(x.reshape(NCHIP, 1, PIECE * WIDTH), CHIPS, 0, 0, tiled=True)
    return pieces.reshape(PAIRS, PROWS, WIDTH)


def scan(core, x, reverse):
    body = functools.partial(scan_kernel, reverse=reverse)
    return call(
        body, "scan", core, [(x, None)], [PAYLOAD], [(0, pieces_block())], backward=reverse
    )[0]


def swap(x):
    return lax.ppermute(x, "c", [(0, 1), (1, 0)])


def shards(queries, keys, values, teacher, query_map, key_map):
    c = lax.axis_index("c").astype(jnp.int32)
    core = c.reshape(1)
    half = HALF * WIDTH

    def others(x):
        part = lax.dynamic_slice(x, (0, (1 - c) * half), (ROWS, half))
        return swap(part.astype(F32))

    k_other, v_other = others(keys), others(values)
    q_other, t_other = others(queries), others(teacher)

    def run(body, name, args, results, groups=GROUPS):
        shapes = [shape for shape, _ in results]
        outs = [(n, spec) for n, (_, spec) in enumerate(results) if spec is not None]
        return call(body, name, core, args, shapes, outs, groups=groups)

    own = group_columns("own")
    cols = group_columns()
    natural = (sds((HALF, TOK, WIDTH), BF16), heads_block(TOK, WIDTH))
    features = (sds((HALF, WIDTH, TOK)), heads_block(WIDTH, TOK))
    row = (sds((HALF, 8, TOK)), heads_block(8, TOK))
    weight = core_heads(64, WIDTH)
    payload = (PAYLOAD, pieces_block())
    lossy = (pltpu.VMEM((8, WIDTH), F32), None)

    halved = (sds((HALF, WIDTH, TOK), BF16), heads_block(WIDTH, TOK))
    swapped = [(keys, own), (k_other, None), (values, own), (v_other, None)]
    phik, send = run(key_kernel, "keys", swapped + [(key_map, weight)], [halved, payload])
    gathered = exchange(send)
    kf, vf = run(pack_kernel, "pack", swapped, [natural, natural])
    gathered, kf, vf, q_other, t_other = lax.optimization_barrier(
        (gathered, kf, vf, q_other, t_other)
    )
    qf, phiq, phiqb, tf, den, num = run(
        score_kernel, "scores",
        [(queries, own), (q_other, cols), (query_map, weight), (phik, halved[1]),
         (vf, natural[1]), (teacher, own), (t_other, cols)],
        [natural, features, natural, natural, row, (pltpu.VMEM((HALF, TOK, WIDTH), F32), None)],
    )
    pre = exchange(scan(core, gathered, False))
    y_own, y_send, dnum, dden, send, loss = run(
        out_kernel, "outs",
        [(pre, None), (num, None), (phiq, features[1]), (phiqb, natural[1]), (den, row[1]),
         (tf, natural[1])],
        [(sds((ROWS, half), BF16), cols), (sds((ROWS, half), BF16), cols), natural, row, payload,
         lossy],
        groups=((6, 10), (4, 4, 4, 2, 2)),
    )
    loss_other = swap(loss)
    gathered = exchange(send)
    query_sent, dphik = run(
        grid_kernel, "grids",
        [(dnum, natural[1]), (vf, natural[1]), (dden, row[1]), (phiq, features[1]),
         (phik, halved[1]), (pre, payload[1]), (qf, natural[1])],
        [(GRADS, quads_block(0)), (pltpu.VMEM((HALF, WIDTH, TOK), F32), None)],
    )
    gathered, dphik, query_sent, y_send = lax.optimization_barrier(
        (gathered, dphik, query_sent, y_send)
    )
    y_other = swap(y_send.astype(F32))
    suf, y_other = lax.optimization_barrier((exchange(scan(core, gathered, True)), y_other))
    send, = call(
        last_kernel, "last", core,
        [(suf, None), (vf, natural[1]), (phik, halved[1]), (kf, natural[1]), (dphik, None),
         (loss, None), (loss_other, None), (query_sent, pltpu.HBM)],
        [GRADS], [(0, quads_block(1))], aliases=[(8, 0)],
    )
    attn, = call(
        merge_kernel, "merge", core, [(y_own, cols), (y_other, None)],
        [sds((ROWS, HEADS * WIDTH), BF16)],
        [(0, own), (0, group_columns("other"))],
    )
    gathered, attn = lax.optimization_barrier((exchange(send), attn))
    spread, = raw_call(
        sum_kernel, "sum", core, [gathered], [None], [PAYLOAD],
        [pltpu.VMEM((PROWS, WIDTH), F32), pltpu.SemaphoreType.DMA((PAIRS,))],
    )
    total = exchange(spread).reshape(GRADS.shape)
    theirs = swap(total)
    loss = jnp.sum(total[0, 1, 32]) * (1.0 / (HEADS * WIDTH) / (NCHIP * TOK))
    grad = sds((HEADS, 64, WIDTH))
    mine, other = core_heads(64, WIDTH), core_heads(64, WIDTH, other=True)
    grad_query, grad_key = call(
        unpack_kernel, "unpack_mine", core, [(total, None)], [grad, grad],
        [(0, mine), (1, mine)],
    )
    grad_query, grad_key = call(
        unpack_kernel, "unpack", core,
        [(theirs, None), (grad_query, pltpu.HBM), (grad_key, pltpu.HBM)], [grad, grad],
        [(0, other), (1, other)], aliases=[(2, 0), (3, 1)],
    )
    return attn, loss, grad_query, grad_key


def solution(mesh):
    fine = Mesh(mesh.devices.reshape(4, 4, 4, 2), ("x", "z", "y", "c"))
    tokens = P(("x", "z", "y", "c"), None)
    return jax.shard_map(
        shards,
        mesh=fine,
        in_specs=(tokens, tokens, tokens, tokens, P(), P()),
        out_specs=(tokens, P(), P(), P()),
        check_vma=False,
    )
```

```python
import functools

import jax
import jax.numpy as jnp
from jax import lax
from jax.experimental import pallas as pl
from jax.experimental.pallas import tpu as pltpu
from jax.sharding import Mesh
from jax.sharding import PartitionSpec as P

F32 = jnp.float32
BF16 = jnp.bfloat16
CHIPS = ("x", "z", "y")
NCHIP = 64
HEADS = 32
HALF = 16
ROWS = 128
TOK = 256
WIDTH = 128
PIECE = 33
PAIRS = HALF // 2
GROUPS = ((8, 8), (4, 4, 4, 4))
PROWS = 2 * 4 * PIECE

NN = ((1,), (0,))
NT = ((1,), (1,))


def dot(a, b, dims=NN):
    return lax.dot_general(a, b, (dims, ((), ())), preferred_element_type=F32)


def two_parts(x):
    high = x.astype(BF16)
    return high, (x - high.astype(F32)).astype(BF16)


def soft_maps(logits):
    e_one = jnp.exp(logits - jnp.max(logits, axis=0, keepdims=True))
    e_two = jnp.exp(jnp.min(logits, axis=0, keepdims=True) - logits)
    one = e_one * (1.0 / jnp.sum(e_one, axis=0, keepdims=True))
    two = e_two * (1.0 / jnp.sum(e_two, axis=0, keepdims=True))
    return jnp.concatenate([one, two], axis=0)


def soft_back(phi, dphi, x, rounded=False):
    halves = []
    for part in (slice(0, 64), slice(64, 128)):
        prod = phi[part] * dphi[part]
        mean = jnp.sum(prod, axis=0, keepdims=True)
        if rounded:
            mean = mean * (1.0 / jnp.sum(phi[part], axis=0, keepdims=True))
        halves.append(prod - phi[part] * mean)
    return dot((halves[0] - halves[1]).astype(BF16), x)


def columns(h):
    return slice(h * WIDTH, (h + 1) * WIDTH)


def both_cores(own, other, h):
    return jnp.concatenate(
        [own[:, columns(h)], other[:, columns(h)].astype(BF16)], axis=0
    )


def put_state(ref, h, state, row):
    pair = h // 2
    for q in range(4):
        at = (4 * (h % 2) + q) * PIECE
        ref[pair, at : at + 32, :] = state[32 * q : 32 * q + 32]
        ref[pair, at + 32 : at + 33, :] = row


def put_grad(ref, h, grad, row):
    for q in range(2):
        at = (2 * (h % 4) + q) * PIECE
        ref[h // 4, at : at + 32, :] = grad[32 * q : 32 * q + 32]
        ref[h // 4, at + 32 : at + 33, :] = row


def get_grad(ref, h, side):
    at = 2 * (h % 4) * PIECE
    parts = [ref[h // 4, side, at + q * PIECE : at + q * PIECE + 32, :] for q in range(2)]
    return jnp.concatenate(parts, axis=0)


def get_state(ref, h):
    first = 4 * (h % 2)
    parts = [ref[h // 2, (first + q) * PIECE : (first + q) * PIECE + 32, :] for q in range(4)]
    at = first * PIECE + 32
    return jnp.concatenate(parts, axis=0), ref[h // 2, at : at + 1, :]


def as_column(row, lanes):
    return jnp.broadcast_to(row, (lanes, row.shape[1])).T


def twice(x):
    return jnp.concatenate([x, x], axis=1)


def causal(core):
    shift = core * ROWS
    at_query = lax.broadcasted_iota(jnp.int32, (TOK, TOK), 0) ^ shift
    at_key = lax.broadcasted_iota(jnp.int32, (TOK, TOK), 1) ^ shift
    return at_query >= at_key


def key_kernel(core, k_own, k_other, v_own, v_other, w_ref, phik_ref, send):
    ones = jnp.ones((8, 2 * TOK), BF16)

    def head(h):
        logits = dot(w_ref[h], both_cores(k_own, k_other, h), NT)
        yield
        phik = soft_maps(logits)
        phikb, low = two_parts(phik)
        phik_ref[h] = phikb
        yield
        state = dot(phikb, both_cores(v_own, v_other, h))
        row = dot(ones, jnp.concatenate([phikb, low], axis=1), NT)[:1]
        yield
        put_state(send, h, state, row)

    return head


def pack_kernel(core, k_own, k_other, v_own, v_other, kf, vf):
    def head(h):
        kf[h] = both_cores(k_own, k_other, h)
        vf[h] = both_cores(v_own, v_other, h)
        yield

    return head


def score_kernel(
    core, q_own, q_other, w_ref, phik_ref, vf, t_own, t_other,
    qf, phiq_ref, phiqb_ref, tf, den_ref, num_ref,
):
    mask = causal(core)
    ones = jnp.ones((8, 2 * TOK), BF16)

    def head(h):
        q = both_cores(q_own, q_other, h)
        qf[h] = q
        logits = dot(w_ref[h], q, NT)
        yield
        phiq = soft_maps(logits)
        phiq_ref[h] = phiq
        phiqb = phiq.astype(BF16).T
        phiqb_ref[h] = phiqb
        tf[h] = both_cores(t_own, t_other, h)
        yield
        scores = dot(phiqb, phik_ref[h])
        yield
        high, low = two_parts(jnp.where(mask, scores, 0.0))
        num_ref[h] = dot(high, vf[h])
        den_ref[h] = dot(ones, jnp.concatenate([high, low], axis=1), NT)

    return head


def out_kernel(
    core, pre, num_ref, phiq_ref, phiqb_ref, den_ref, tf,
    y_own, y_send, dnum_ref, dden_ref, send, loss_ref,
):
    ones = jnp.ones((8, 2 * WIDTH), BF16)
    wide = jnp.ones((8, 2 * TOK), BF16)
    scale = 2.0 / (HEADS * WIDTH)
    loss_ref[...] = jnp.zeros_like(loss_ref)

    def head(h):
        state, norm = get_state(pre, h)
        carried = dot(phiqb_ref[h], state.astype(BF16))
        down = as_column(norm, WIDTH)
        yield
        phiq = phiq_ref[h]
        before = jnp.sum(phiq * twice(down), axis=0, keepdims=True)
        inv = as_column(1.0 / (den_ref[h][:1] + before), WIDTH)
        yield
        y = (num_ref[h] + carried) * inv
        y_own[:, columns(h)] = y[:ROWS].astype(BF16)
        y_send[:, columns(h)] = y[ROWS:].astype(BF16)
        err = y - tf[h].astype(F32)
        loss_ref[...] += jnp.sum((err * err).reshape(TOK // 8, 8, WIDTH), axis=0)
        dnum = (scale * err) * inv
        dnumb = dnum.astype(BF16)
        dnum_ref[h] = dnumb
        high, low = two_parts(dnum * y)
        both = jnp.concatenate([high, low], axis=1)
        yield
        dden = -dot(ones, both, NT)
        rev = dot(phiq_ref[h].astype(BF16), dnumb)
        yield
        dden_ref[h] = dden
        high, low = two_parts(phiq_ref[h] * dden[:1])
        yield
        rnorm = dot(wide, jnp.concatenate([high, low], axis=1), NT)
        yield
        put_state(send, h, rev, rnorm[:1])

    return head


def grid_kernel(
    core, dnum_ref, vf, dden_ref, phiq_ref, phik_ref, pre, qf, send, dphik_ref,
):
    mask = causal(core)

    def head(h):
        grid = dot(dnum_ref[h], vf[h], NT)
        column = as_column(dden_ref[h][:1], WIDTH)
        yield
        gridb = jnp.where(mask, grid + twice(column), 0.0).astype(BF16)
        dphik_ref[h] = dot(phiq_ref[h].astype(BF16), gridb)
        state, norm = get_state(pre, h)
        left = jnp.concatenate([phik_ref[h], state.astype(BF16)], axis=1)
        dphiq = dot(left, jnp.concatenate([gridb, dnum_ref[h]], axis=1), NT)
        down = twice(as_column(norm, WIDTH))
        yield
        grad = soft_back(phiq_ref[h], dphiq + down * dden_ref[h][:1], qf[h])
        put_grad(send, h, grad, jnp.zeros((1, WIDTH), F32))

    return head


def merge_kernel(core, y_own, y_other, attn_mine, attn_theirs):
    del core

    def head(h):
        attn_mine[:, columns(h)] = y_own[:, columns(h)]
        attn_theirs[:, columns(h)] = y_other[:, columns(h)].astype(BF16)
        yield

    return head


def last_kernel(
    core, suf, vf, phik_ref, kf, dphik_ref, loss_ref, loss_other, queries_sent, send
):
    del queries_sent
    row = jnp.sum(loss_ref[...] + loss_other[...], axis=0, keepdims=True)

    def head(h):
        state, norm = get_state(suf, h)
        carried = dot(state.astype(BF16), vf[h], NT) + twice(as_column(norm, WIDTH))
        yield
        grad_key = soft_back(
            phik_ref[h].astype(F32), dphik_ref[h] + carried, kf[h], rounded=True
        )
        yield
        put_grad(send, h, grad_key, row)

    return head


def scan_kernel(core, x_ref, o_ref, *, reverse):
    del core
    acc = jnp.zeros((PIECE, WIDTH), F32)

    def head(h):
        nonlocal acc
        for j in range(3, -1, -1) if reverse else range(4):
            at = (4 * (h % 2) + j) * PIECE
            o_ref[h // 2, at : at + PIECE, :] = acc
            acc = acc + x_ref[h // 2, at : at + PIECE, :]
        yield

    return head


def sum_kernel(core_ref, x_ref, o_ref, buf, sems):
    del core_ref
    parts = []
    for b in range(PAIRS):
        part = x_ref[b, :PIECE, :]
        for j in range(1, 8):
            part = part + x_ref[b, PIECE * j : PIECE * (j + 1), :]
        parts.append(part)
    while len(parts) > 1:
        parts = [x + y for x, y in zip(parts[::2], parts[1::2])]
    for j in range(8):
        buf[PIECE * j : PIECE * (j + 1), :] = parts[0]
    copies = [pltpu.make_async_copy(buf, o_ref.at[b], sems.at[b]) for b in range(PAIRS)]
    for copy in copies:
        copy.start()
    for copy in copies:
        copy.wait()


def unpack_kernel(core, *refs):
    del core
    src, gq, gk = refs[0], refs[-2], refs[-1]

    def head(h):
        gq[h] = get_grad(src, h, 0)
        gk[h] = get_grad(src, h, 1)
        yield

    return head


class Block:
    def __init__(self, shape, view, cut=None):
        self.shape = shape
        self.view = view
        self.cut = cut or (lambda ref, core, start, count: view(ref, start, count))


def heads_block(*tail):
    return Block((HALF,) + tail, lambda ref, start, count: ref.at[pl.ds(start, count)])


def core_heads(*tail, other=False):
    def cut(ref, core, start, count):
        return ref.at[pl.ds(((1 - core) if other else core) * HALF + start, count)]

    return Block((HALF,) + tail, heads_block(*tail).view, cut)


def group_columns(core_part=None):
    def view(ref, start, count):
        return ref.at[:, pl.ds(start * WIDTH, count * WIDTH)]

    def cut(ref, core, start, count):
        side = core if core_part == "own" else 1 - core
        at = pl.multiple_of(side * HALF * WIDTH + start * WIDTH, WIDTH)
        return ref.at[:, pl.ds(at, count * WIDTH)]

    return Block((ROWS, HALF * WIDTH), view, cut if core_part else None)


def pieces_block():
    def view(ref, start, count):
        return ref.at[pl.ds(start // 2, count // 2)]

    return Block((PAIRS, PROWS, WIDTH), view)


def is_block(spec):
    return isinstance(spec, Block)


def stream(*refs, body, ins, outs, n_out, groups, backward):
    core = refs[0][0]
    arrays = refs[1 : 1 + len(ins)]
    results = refs[1 + len(ins) : 1 + len(ins) + n_out]
    in_sems, out_sems, *buffers = refs[1 + len(ins) + n_out :]
    given = [buffers.pop(0) if is_block(spec) else ref for spec, ref in zip(ins, arrays)]
    streamed = [at for at, _ in outs]
    whole = [ref for n, ref in enumerate(results) if n not in streamed]
    heads = list(range(HALF))
    if backward:
        heads.reverse()

    def spans_of(counts):
        spans = []
        for g, count in enumerate(counts):
            part = heads[sum(counts[:g]) : sum(counts[:g]) + count]
            spans.append((min(part), count))
        return spans

    spans_in, spans_out = spans_of(groups[0]), spans_of(groups[1])

    def copies_in(g):
        return [
            pltpu.make_async_copy(
                spec.cut(ref, core, *spans_in[g]), spec.view(buf, *spans_in[g]), in_sems.at[n, g]
            )
            for n, (spec, ref, buf) in enumerate(zip(ins, arrays, given))
            if is_block(spec)
        ]

    def copies_out(g):
        return [
            pltpu.make_async_copy(
                spec.view(buf, *spans_out[g]),
                spec.cut(results[at], core, *spans_out[g]),
                out_sems.at[n, g],
            )
            for n, ((at, spec), buf) in enumerate(zip(outs, buffers))
        ]

    for g in range(len(spans_in)):
        for copy in copies_in(g):
            copy.start()
    head = body(core, *given, *buffers, *whole)
    done = 0
    ends = [sum(groups[1][: g + 1]) for g in range(len(spans_out))]

    running = []

    def advance():
        nonlocal done
        for item in list(running):
            if next(item, "end") == "end":
                running.remove(item)
                done += 1
                if done in ends:
                    for copy in copies_out(ends.index(done)):
                        copy.start()

    for g, (_, count) in enumerate(spans_in):
        for copy in copies_in(g):
            copy.wait()
        for _ in range(count):
            running.append(head(heads.pop(0)))
            advance()
    while running:
        advance()
    for g in range(len(spans_out)):
        for copy in copies_out(g):
            copy.wait()


def quads_block(side):
    def view(ref, start, count):
        return ref.at[pl.ds(start // 4, count // 4)]

    def cut(ref, core, start, count):
        return ref.at[pl.ds(start // 4, count // 4), side]

    return Block((HALF // 4, PROWS, WIDTH), view, cut)


def raw_call(body, name, core, values, specs, shapes, scratch, aliases=()):
    spaces = {None: pltpu.VMEM}
    constrained = [
        pltpu.with_memory_space_constraint(v, spaces.get(s, pltpu.HBM))
        for v, s in zip(values, specs)
    ]
    return pl.pallas_call(
        body,
        in_specs=[pl.BlockSpec(memory_space=pltpu.SMEM)]
        + [pl.BlockSpec(memory_space=spaces.get(s, pltpu.HBM)) for s in specs],
        out_specs=tuple(pl.BlockSpec(memory_space=shape.memory_space) for shape in shapes),
        out_shape=tuple(shapes),
        scratch_shapes=scratch,
        name=name,
        input_output_aliases=dict(aliases),
        compiler_params=pltpu.CompilerParams(vmem_limit_bytes=48 * 1024 * 1024),
    )(core, *constrained)


def call(
    body, name, core, args, shapes, outs, aliases=(), groups=GROUPS, backward=False
):
    ins = [spec for _, spec in args]
    scratch = [
        pltpu.SemaphoreType.DMA((len(ins), len(groups[0]))),
        pltpu.SemaphoreType.DMA((len(outs), len(groups[1]))),
    ]
    scratch += [pltpu.VMEM(spec.shape, value.dtype) for value, spec in args if is_block(spec)]
    scratch += [pltpu.VMEM(spec.shape, shapes[at].dtype) for at, spec in outs]
    kernel = functools.partial(
        stream, body=body, ins=ins, outs=outs, n_out=len(shapes), groups=groups,
        backward=backward,
    )
    return raw_call(kernel, name, core, [v for v, _ in args], ins, shapes, scratch, aliases)


def sds(shape, dtype=F32):
    return pltpu.HBM(shape, dtype)


PAYLOAD = sds((PAIRS, PROWS, WIDTH))


GRADS = sds((HALF // 4, 2, PROWS, WIDTH))


def exchange(x):
    pieces = lax.all_to_all(x.reshape(NCHIP, 1, PIECE * WIDTH), CHIPS, 0, 0, tiled=True)
    return pieces.reshape(PAIRS, PROWS, WIDTH)


def scan(core, x, reverse):
    body = functools.partial(scan_kernel, reverse=reverse)
    return call(
        body, "scan", core, [(x, None)], [PAYLOAD], [(0, pieces_block())], backward=reverse
    )[0]


def swap(x):
    return lax.ppermute(x, "c", [(0, 1), (1, 0)])


def shards(queries, keys, values, teacher, query_map, key_map):
    c = lax.axis_index("c").astype(jnp.int32)
    core = c.reshape(1)
    half = HALF * WIDTH

    def others(x):
        part = lax.dynamic_slice(x, (0, (1 - c) * half), (ROWS, half))
        return swap(part.astype(F32))

    k_other, v_other = others(keys), others(values)
    q_other, t_other = others(queries), others(teacher)

    def run(body, name, args, results, groups=GROUPS):
        shapes = [shape for shape, _ in results]
        outs = [(n, spec) for n, (_, spec) in enumerate(results) if spec is not None]
        return call(body, name, core, args, shapes, outs, groups=groups)

    own = group_columns("own")
    cols = group_columns()
    natural = (sds((HALF, TOK, WIDTH), BF16), heads_block(TOK, WIDTH))
    features = (sds((HALF, WIDTH, TOK)), heads_block(WIDTH, TOK))
    row = (sds((HALF, 8, TOK)), heads_block(8, TOK))
    weight = core_heads(64, WIDTH)
    payload = (PAYLOAD, pieces_block())
    lossy = (pltpu.VMEM((8, WIDTH), F32), None)

    halved = (sds((HALF, WIDTH, TOK), BF16), heads_block(WIDTH, TOK))
    swapped = [(keys, own), (k_other, None), (values, own), (v_other, None)]
    phik, send = run(key_kernel, "keys", swapped + [(key_map, weight)], [halved, payload])
    gathered = exchange(send)
    kf, vf = run(pack_kernel, "pack", swapped, [natural, natural])
    gathered, kf, vf, q_other, t_other = lax.optimization_barrier(
        (gathered, kf, vf, q_other, t_other)
    )
    qf, phiq, phiqb, tf, den, num = run(
        score_kernel, "scores",
        [(queries, own), (q_other, cols), (query_map, weight), (phik, halved[1]),
         (vf, natural[1]), (teacher, own), (t_other, cols)],
        [natural, features, natural, natural, row, (pltpu.VMEM((HALF, TOK, WIDTH), F32), None)],
    )
    pre = exchange(scan(core, gathered, False))
    y_own, y_send, dnum, dden, send, loss = run(
        out_kernel, "outs",
        [(pre, None), (num, None), (phiq, features[1]), (phiqb, natural[1]), (den, row[1]),
         (tf, natural[1])],
        [(sds((ROWS, half), BF16), cols), (sds((ROWS, half), BF16), cols), natural, row, payload,
         lossy],
        groups=((4, 4, 8), (4, 4, 4, 2, 2)),
    )
    loss_other = swap(loss)
    gathered = exchange(send)
    query_sent, dphik = run(
        grid_kernel, "grids",
        [(dnum, natural[1]), (vf, natural[1]), (dden, row[1]), (phiq, features[1]),
         (phik, halved[1]), (pre, payload[1]), (qf, natural[1])],
        [(GRADS, quads_block(0)), (pltpu.VMEM((HALF, WIDTH, TOK), F32), None)],
    )
    gathered, dphik, query_sent, y_send = lax.optimization_barrier(
        (gathered, dphik, query_sent, y_send)
    )
    y_other = swap(y_send.astype(F32))
    suf, y_other = lax.optimization_barrier((exchange(scan(core, gathered, True)), y_other))
    send, = call(
        last_kernel, "last", core,
        [(suf, None), (vf, natural[1]), (phik, halved[1]), (kf, natural[1]), (dphik, None),
         (loss, None), (loss_other, None), (query_sent, pltpu.HBM)],
        [GRADS], [(0, quads_block(1))], aliases=[(8, 0)], groups=((4, 4, 8), (4, 4, 4, 4)),
    )
    attn, = call(
        merge_kernel, "merge", core, [(y_own, cols), (y_other, None)],
        [sds((ROWS, HEADS * WIDTH), BF16)],
        [(0, own), (0, group_columns("other"))],
    )
    gathered, attn = lax.optimization_barrier((exchange(send), attn))
    spread, = raw_call(
        sum_kernel, "sum", core, [gathered], [None], [PAYLOAD],
        [pltpu.VMEM((PROWS, WIDTH), F32), pltpu.SemaphoreType.DMA((PAIRS,))],
    )
    total = exchange(spread).reshape(GRADS.shape)
    theirs = swap(total)
    loss = jnp.sum(total[0, 1, 32]) * (1.0 / (HEADS * WIDTH) / (NCHIP * TOK))
    grad = sds((HEADS, 64, WIDTH))
    mine, other = core_heads(64, WIDTH), core_heads(64, WIDTH, other=True)
    grad_query, grad_key = call(
        unpack_kernel, "unpack_mine", core, [(total, None)], [grad, grad],
        [(0, mine), (1, mine)],
    )
    grad_query, grad_key = call(
        unpack_kernel, "unpack", core,
        [(theirs, None), (grad_query, pltpu.HBM), (grad_key, pltpu.HBM)], [grad, grad],
        [(0, other), (1, other)], aliases=[(2, 0), (3, 1)],
    )
    return attn, loss, grad_query, grad_key


def solution(mesh):
    fine = Mesh(mesh.devices.reshape(4, 4, 4, 2), ("x", "z", "y", "c"))
    tokens = P(("x", "z", "y", "c"), None)
    return jax.shard_map(
        shards,
        mesh=fine,
        in_specs=(tokens, tokens, tokens, tokens, P(), P()),
        out_specs=(tokens, P(), P(), P()),
        check_vma=False,
    )
```
